512 devices in a mesh: va: 32 (over x_lo, y, core), vb: 16 (over x_hi, z).
Axes of the slice: x: 4 (x_hi: 2, x_lo: 2; x = x_hi * 2 + x_lo), y: 8, z: 8, core: 2. Of those that a mesh axis runs over, the one named last changes fastest.
Arguments:
- amplitudes: bfloat16 [1024, 8, 65536], P('va', None, 'vb'), may hold values from -6 to 6
- integrals: bfloat16 [1024, 65536], P('va', 'vb'), may hold values from -0.125 to 0.125
- irrep_virt: int32 [1024], replicated, may hold values from 0 to 7
- irrep_occ: int32 [64], replicated, may hold values from 0 to 7, as said below
- irrep_slab: int32 [8], replicated, may hold values from 0 to 7
Outputs:
- cycle_term: bfloat16 [1024, 8192], P('vb', 'va')
The draws below stay inside these ranges and needn't reach their ends.
Inputs may be any that keep to these rules, and one draw needn't show every extreme that they name: `irrep_virt`: D2h irrep labels. `irrep_occ`: D2h irrep labels; each aligned group of 8 consecutive orbitals k holds every label exactly once. `irrep_slab`: D2h irrep labels.
All inputs are finite; a program needn't handle non-finite values.
Results may differ from the reference program's by a relative error of at most 0.0015.
Values may be sent and summed in bfloat16 or wider, within the bound.
No kernel may reach another device: no remote copies, remote signals or barrier semaphores. Data moves between devices by JAX's collectives and lax.ppermute only.
A program may use at most 64 MiB of HBM per device.

```python
import jax
import jax.numpy as jnp
from jax import lax

V = 1024
K = 64
I_SL = 8
VK = 65536


def draw_irrep_occ(key, part):
    group_keys = jax.random.split(jax.random.fold_in(key, 17), K // 8)
    labels = jax.vmap(lambda one_key: jax.random.permutation(one_key, 8))(group_keys)
    return labels.reshape(K).astype(jnp.int32)


def set_ends(values, rng, least, largest):
    longest = values.shape.index(max(values.shape))
    spots = []
    for shift in (0, 1):
        where = [jax.random.randint(jax.random.fold_in(rng, axis), (), 0, length) for axis, length in enumerate(values.shape)]
        where[longest] = (where[longest] + shift) % values.shape[longest]
        spots.append(tuple(where))
    return values.at[spots[0]].set(least).at[spots[1]].set(largest)


def spiked(entries, own_key, source, target, shards_of, factor):
    owner, partner = [(jnp.arange(entries.shape[dim]) // (entries.shape[dim] // shards_of)).reshape([-1 if axis == dim else 1 for axis in range(entries.ndim)]) for dim in (source, target)]
    chosen = jax.random.permutation(own_key, shards_of)[partner]
    strong = (owner == chosen) | (owner == (partner + shards_of // 2) % shards_of)
    return jnp.where(strong, factor * entries, entries)


def block_scale(own_key, shape, cuts, smallest, top_value):
    factor_of, own = 1.0, jax.random.fold_in(own_key, 6)
    for dim, parts in cuts:
        draws = jnp.exp(jax.random.uniform(jax.random.fold_in(own, dim), (parts,), jnp.float32, smallest / len(cuts), top_value / len(cuts)))
        factor_of = factor_of * jnp.repeat(draws, shape[dim] // parts).reshape([-1 if axis == dim else 1 for axis in range(len(shape))])
    return factor_of


def bell_draw(stream_key, extent, spread, bound, shards=(), kind=jnp.bfloat16):
    entries = jax.random.normal(stream_key, extent, jnp.float32) * spread
    if len(shards) > 0:
        entries = block_scale(stream_key, extent, shards, -0.22, 0.18) * entries
    return jnp.clip(entries, min=-bound, max=bound).astype(kind)


def gaussian_with(rng, extent, width, reach, pieces, heavy, held_as=jnp.bfloat16):
    drawn = width * jax.random.normal(rng, extent, jnp.float32)
    if pieces:
        drawn = drawn * block_scale(rng, extent, pieces, -0.22, 0.18)
    return jnp.clip(spiked(drawn, jax.random.fold_in(rng, 3), *heavy), -reach, reach).astype(held_as)


def setup_inputs(seed: int = 0) -> dict:
    splits = jax.random.split(jax.random.key(seed), 6)
    return {
        "amplitudes": bell_draw(splits[0], (V, I_SL, VK), 1.0, 6.0, ((0, 32), (2, 16))),
        "integrals": gaussian_with(splits[1], (V, VK), (V * K // 8) ** -0.5, 0.125, ((0, 32), (1, 16)), (1, 0, 32, 2.75)),
        "irrep_virt": set_ends(jax.random.randint(splits[2], (V,), 0, 8), jax.random.fold_in(splits[2], 1), 0, 7).astype(jnp.int32),
        "irrep_occ": draw_irrep_occ(jax.random.fold_in(splits[5], 71), 0),
        "irrep_slab": set_ends(jax.random.randint(splits[4], (I_SL,), 0, 8), jax.random.fold_in(splits[4], 1), 0, 7).astype(jnp.int32),
    }


def reference(amplitudes, integrals, irrep_virt, irrep_occ, irrep_slab):
    pair_tag = jnp.bitwise_xor(irrep_virt[:, None], irrep_occ[None, :]).reshape(V * K)
    row_tag = jnp.bitwise_xor(irrep_virt, irrep_occ[0])
    int_sym = jnp.where(row_tag[:, None] == pair_tag[None, :], integrals, jnp.zeros_like(integrals))
    block_size = 32
    block_total = V // block_size

    def one_block(block_index):
        first_row = (block_index * block_size).astype(jnp.int32)
        amp_block = lax.dynamic_slice_in_dim(amplitudes, first_row, block_size, 0)
        virt_block = lax.dynamic_slice_in_dim(irrep_virt, first_row, block_size, 0)
        left_tag = jnp.bitwise_xor(virt_block[:, None], irrep_slab[None, :])
        amp_sym = jnp.where(left_tag[:, :, None] == pair_tag[None, None, :], amp_block, jnp.zeros_like(amp_block))
        flat_amp = amp_sym.reshape(block_size * I_SL, V * K)
        return lax.dot_general(int_sym, flat_amp, (((1,), (1,)), ((), ())), preferred_element_type=jnp.float32)

    blocks = lax.map(one_block, jnp.arange(block_total, dtype=jnp.int32))
    cycle_term = jnp.transpose(blocks, (1, 0, 2)).reshape(V, V * I_SL)
    return cycle_term.astype(jnp.bfloat16)
```

```python
import functools

import jax
import jax.numpy as jnp
from jax import lax
from jax.experimental import pallas as pl
from jax.experimental.pallas import tpu as pltpu
from jax.sharding import Mesh, PartitionSpec as P

GROUP = 8
LANES = 128
WINDOW = 64
SLOTS = 24
BIG = 100 << 20

F32, BF16, I32 = jnp.float32, jnp.bfloat16, jnp.int32
SMEM = pl.BlockSpec(memory_space=pltpu.SMEM)
VMEM = pl.BlockSpec(memory_space=pltpu.VMEM)


def params(**more):
    return pltpu.CompilerParams(vmem_limit_bytes=48 << 20, **more)


def lanes(shape):
    return lax.broadcasted_iota(I32, shape, len(shape) - 1)


def rows_of(shape):
    return lax.broadcasted_iota(I32, shape, len(shape) - 2)


def spread(ref, start, count, position):
    out = jnp.zeros_like(position)
    for n in range(count):
        out = jnp.where(position == n, ref[start + n], out)
    return out


def occ_lanes(occ_ref):
    occ_count = occ_ref.shape[0]
    return spread(occ_ref, 0, occ_count, lanes((1, LANES)) % occ_count)


def pair_tags(occ, virt_ref, first_c, block, occ_count):
    per = LANES // occ_count
    c_of = lanes((1, LANES)) // occ_count
    return occ ^ spread(virt_ref, first_c + block * per, per, c_of)


def squeezer(width):
    shape = (width, width // GROUP)
    return jnp.where(rows_of(shape) // GROUP == lanes(shape), 1.0, 0.0).astype(BF16)


def first_of(axis_sizes):
    at = 0
    for name, size in axis_sizes:
        at = at * size + lax.axis_index(name)
    return at


def squeeze_int_kernel(va_axes, vb_axes, virt_ref, occ_ref, int_ref, out_ref):
    row_count, width = int_ref.shape
    occ_count = occ_ref.shape[0]
    c_count = width // occ_count
    va, vb = first_of(va_axes), first_of(vb_axes)
    occ = occ_lanes(occ_ref)
    row_tag = spread(virt_ref, va * row_count, row_count, rows_of((row_count, LANES))) ^ occ_ref[0]
    step = GROUP * LANES
    squeeze = squeezer(step)
    for part in range(width // step):
        kept = []
        for block in range(GROUP):
            at = part * GROUP + block
            tag = pair_tags(occ, virt_ref, vb * c_count, at, occ_count)
            held = int_ref[:, at * LANES : (at + 1) * LANES].astype(F32)
            kept.append(jnp.where(row_tag == tag, held, 0.0).astype(BF16))
        small = jnp.dot(jnp.concatenate(kept, 1), squeeze, preferred_element_type=F32).astype(BF16)
        for peer in range(out_ref.shape[0]):
            out_ref[peer, :, part * LANES : (part + 1) * LANES] = small


def squeeze_amp_kernel(va_axes, vb_axes, virt_ref, occ_ref, slab_ref, labels_ref, amp_ref, out_ref, most_ref):
    a_count, slab_count, width = amp_ref.shape
    occ_count = occ_ref.shape[0]
    part = pl.program_id(0)
    c_count = width // occ_count * pl.num_programs(0)
    va, vb = first_of(va_axes), first_of(vb_axes)
    occ = occ_lanes(occ_ref)
    slab = spread(slab_ref, 0, slab_count, rows_of((slab_count, LANES)))
    left = jnp.stack([slab ^ virt_ref[va * a_count + a] for a in range(a_count)])
    kept = []
    for block in range(GROUP):
        tag = pair_tags(occ, virt_ref, vb * c_count, part * GROUP + block, occ_count)
        held = amp_ref[:, :, block * LANES : (block + 1) * LANES].astype(F32)
        kept.append(jnp.where(left == tag[None], held, 0.0).reshape(a_count * slab_count, LANES).astype(BF16))
    out_ref[...] = jnp.dot(jnp.concatenate(kept, 1), squeezer(width), preferred_element_type=F32).astype(BF16)

    @pl.when(part == 0)
    def _():
        labels = labels_ref[...]
        half = lanes(labels.shape) // WINDOW
        most = jnp.int32(0)
        for label in range(GROUP):
            for side in range(LANES // WINDOW):
                hits = jnp.where((labels == label) & (half == side), 1, 0)
                most = jnp.maximum(most, jnp.max(jnp.sum(hits, axis=1, keepdims=True)))
        most_ref[0] = most


def sort_keys(labels):
    at = lanes(labels.shape)
    return (at // WINDOW) * (WINDOW * GROUP) + labels * WINDOW + at % WINDOW


def column_tags(va_axes, virt_ref, slab_ref, occ_ref, a_count):
    slab_count = slab_ref.shape[0]
    at = lanes((1, a_count * slab_count))
    first = spread(virt_ref, first_of(va_axes) * a_count, a_count, at // slab_count)
    return first ^ spread(slab_ref, 0, slab_count, at % slab_count) ^ occ_ref[0]


def multiply_kernel(slots, va_axes, virt_ref, occ_ref, slab_ref, labels_ref, own_ref, other_ref, amp_ref, out_ref, sorted_ref, tag_ref):
    windows, half_rows, depth = own_ref.shape
    core = lax.axis_index("c")
    columns = column_tags(va_axes, virt_ref, slab_ref, occ_ref, amp_ref.shape[0] // slab_ref.shape[0])
    labels = labels_ref[...]
    keys = sort_keys(labels)
    keys_down = jnp.transpose(keys.astype(F32))
    swap = (lanes(keys.shape) // half_rows) % 2 == 0
    def own_first(x):
        x = x.astype(F32)
        swapped = jnp.where(swap, pltpu.roll(x, LANES - half_rows, 1), pltpu.roll(x, half_rows, 1))
        return jnp.where(core == 0, x, swapped)
    keys_across, labels_across = own_first(keys), own_first(labels)
    square = (LANES, LANES)
    per = LANES // WINDOW
    for r in range(windows // per):
        before = jnp.where(keys_down[:, r : r + 1] < keys_across[r : r + 1, :], 1.0, 0.0)
        place = jnp.sum(before, axis=0, keepdims=True)
        moved = jnp.where(rows_of(square).astype(F32) == place, 1.0, 0.0)
        block = jnp.concatenate([x for w in range(r * per, (r + 1) * per) for x in (own_ref[w], other_ref[w])], 0)
        span = slice(r * LANES, (r + 1) * LANES)
        sorted_ref[span, :] = jnp.dot(moved.astype(BF16), block, preferred_element_type=F32).astype(BF16)
        tag_ref[span, :] = jnp.broadcast_to(
            jnp.sum(moved * labels_across[r : r + 1, :], axis=1, keepdims=True), square
        ).astype(I32)
    for r in range(windows // per):
        span = slice(r * LANES, (r + 1) * LANES)
        sums = lax.dot_general(
            sorted_ref[span, :], amp_ref[...], (((1,), (1,)), ((), ())), preferred_element_type=F32
        )
        tags = jnp.concatenate([tag_ref[span, :]] * (amp_ref.shape[0] // LANES), 1)
        sums = jnp.where(tags == columns, sums, 0.0)
        for w in range(per):
            part = sums[w * WINDOW : (w + 1) * WINDOW]
            total = part[:slots]
            for low in range(slots, WINDOW, slots):
                more = part[low : low + slots]
                if more.shape[0] < slots:
                    more = jnp.concatenate([more, jnp.zeros((slots - more.shape[0], more.shape[1]), F32)], 0)
                total = total + more
            out_ref[r * per + w] = total


def finish_kernel(slots, va_axes, vb_axes, virt_ref, occ_ref, slab_ref, labels_ref, parts_ref, out_ref):
    columns = column_tags(va_axes, virt_ref, slab_ref, occ_ref, out_ref.shape[1] // slab_ref.shape[0])
    vb = first_of(vb_axes)
    per = LANES // WINDOW
    total = parts_ref[0]
    for part in range(1, parts_ref.shape[0]):
        total = total + parts_ref[part]
    total = total.astype(BF16)
    row = labels_ref[pl.ds(vb // per, 1), :]
    mine = lanes(row.shape) // WINDOW == vb % per
    key = jnp.where(mine, row * WINDOW + lanes(row.shape) % WINDOW, WINDOW * GROUP).astype(F32)
    own = jnp.where(mine, lanes(row.shape) % WINDOW, -1)
    shape = (WINDOW, LANES)
    on_own = rows_of(shape) == own
    key_down = jnp.sum(jnp.where(on_own, key, 0.0), axis=1, keepdims=True)
    label_down = jnp.sum(jnp.where(on_own, row.astype(F32), 0.0), axis=1, keepdims=True).astype(I32)
    place = jnp.sum(jnp.where(key < key_down, 1.0, 0.0), axis=1, keepdims=True).astype(I32)
    pick = (WINDOW, slots)
    slot = jnp.where(place >= 2 * slots, place - 2 * slots, jnp.where(place >= slots, place - slots, place))
    chosen = jnp.where(lanes(pick) == slot, 1.0, 0.0).astype(BF16)
    full = jnp.dot(chosen, total, preferred_element_type=F32)
    out_ref[...] = jnp.where(label_down == columns, full, 0.0).astype(BF16)


def per_device(sizes, amplitudes, integrals, irrep_virt, irrep_occ, irrep_slab):
    va_axes = [(name, sizes[name]) for name in ("xl", "y", "c")]
    vb_axes = [(name, sizes[name]) for name in ("xh", "z")]
    a_rows, slab_count, width = amplitudes.shape
    b_rows = integrals.shape[0]
    depth = width // GROUP
    chips = sizes["xl"] * sizes["y"]
    labels = irrep_virt.reshape(-1, LANES)
    columns = a_rows * slab_count

    small = pl.pallas_call(
        functools.partial(squeeze_int_kernel, va_axes, vb_axes),
        out_shape=jax.ShapeDtypeStruct((chips, b_rows, depth), BF16),
        in_specs=[SMEM, SMEM, VMEM],
        out_specs=VMEM,
        compiler_params=params(),
        name="squeeze_int",
    )(irrep_virt, irrep_occ, integrals)
    own = lax.all_to_all(small, ("xl", "y"), 0, 0, tiled=False)
    other = lax.ppermute(own, "c", [(0, 1), (1, 0)])

    step = GROUP * LANES
    amp_small, most = pl.pallas_call(
        functools.partial(squeeze_amp_kernel, va_axes, vb_axes),
        grid=(width // step,),
        out_shape=(jax.ShapeDtypeStruct((columns, depth), BF16), jax.ShapeDtypeStruct((1,), I32)),
        in_specs=[SMEM, SMEM, SMEM, VMEM, pl.BlockSpec((a_rows, slab_count, step), lambda p: (0, 0, p))],
        out_specs=(pl.BlockSpec((columns, LANES), lambda p: (0, p)), SMEM),
        compiler_params=params(),
        name="squeeze_amp",
    )(irrep_virt, irrep_occ, irrep_slab, labels, amplitudes)

    def rest(slots, virt, occ, slab, labels, own, other, amp_small):
        parts = pl.pallas_call(
            functools.partial(multiply_kernel, slots, va_axes),
            out_shape=jax.ShapeDtypeStruct((chips, slots, columns), F32),
            in_specs=[SMEM, SMEM, SMEM] + [VMEM] * 4,
            out_specs=VMEM,
            scratch_shapes=[pltpu.VMEM((chips * WINDOW, depth), BF16), pltpu.VMEM((chips * WINDOW, LANES), I32)],
            compiler_params=params(),
            name="multiply",
        )(virt, occ, slab, labels, own, other, amp_small)
        parts = lax.all_to_all(parts, ("xh", "z"), 0, 0, tiled=False)
        return pl.pallas_call(
            functools.partial(finish_kernel, slots, va_axes, vb_axes),
            out_shape=jax.ShapeDtypeStruct((WINDOW, columns), BF16),
            in_specs=[SMEM, SMEM, SMEM] + [VMEM] * 2,
            out_specs=VMEM,
            compiler_params=params(),
            name="finish",
        )(virt, occ, slab, labels, parts)

    return lax.cond(
        most[0] <= SLOTS,
        functools.partial(rest, SLOTS),
        functools.partial(rest, WINDOW),
        irrep_virt, irrep_occ, irrep_slab, labels, own, other, amp_small,
    )


def solution(mesh):
    names = ("xl", "y", "c", "xh", "z")
    shape = (2, mesh.shape["va"] // 4, 2, 2, mesh.shape["vb"] // 2)
    fine = Mesh(mesh.devices.reshape(shape), names)
    va, vb = names[:3], names[3:]
    return jax.shard_map(
        functools.partial(per_device, dict(zip(names, shape))),
        mesh=fine,
        in_specs=(P(va, None, vb), P(va, vb), P(), P(), P()),
        out_specs=P(vb, va),
        check_vma=False,
    )
```

```python
import functools

import jax
import jax.numpy as jnp
from jax import lax
from jax.experimental import pallas as pl
from jax.experimental.pallas import tpu as pltpu
from jax.sharding import Mesh, PartitionSpec as P

GROUP = 8
LANES = 128
ROOTS = 4
TOP = 7.0
SMALLEST = 2.0**-100
WINDOW = 64
SLOTS = 24

F32, BF16, I32 = jnp.float32, jnp.bfloat16, jnp.int32
SMEM = pl.BlockSpec(memory_space=pltpu.SMEM)
VMEM = pl.BlockSpec(memory_space=pltpu.VMEM)
HBM = pl.BlockSpec(memory_space=pltpu.HBM)
ANY = pl.BlockSpec(memory_space=pl.ANY)


def params(**more):
    return pltpu.CompilerParams(vmem_limit_bytes=48 << 20, **more)


def lanes(shape):
    return lax.broadcasted_iota(I32, shape, len(shape) - 1)


def rows_of(shape):
    return lax.broadcasted_iota(I32, shape, len(shape) - 2)


def spread(ref, start, count, position):
    out = jnp.zeros_like(position)
    for n in range(count):
        out = jnp.where(position == n, ref[start + n], out)
    return out


def occ_lanes(occ_ref):
    occ_count = occ_ref.shape[0]
    return spread(occ_ref, 0, occ_count, lanes((1, LANES)) % occ_count)


def pair_tags(occ, virt_ref, first_c, block, occ_count):
    per = LANES // occ_count
    c_of = lanes((1, LANES)) // occ_count
    return occ ^ spread(virt_ref, first_c + block * per, per, c_of)


def squeezer(width):
    shape = (width, width // GROUP)
    return jnp.where(rows_of(shape) // GROUP == lanes(shape), 1.0, 0.0).astype(BF16)


def first_of(axis_sizes):
    at = 0
    for name, size in axis_sizes:
        at = at * size + lax.axis_index(name)
    return at


def squeeze_int_kernel(va_axes, vb_axes, virt_hbm, occ_hbm, int_hbm, out_hbm, virt_ref, occ_ref, int_ref, small_ref, sems):
    row_count, width = int_ref.shape
    occ_count = occ_ref.shape[0]
    c_count = width // occ_count
    step = GROUP * LANES
    parts = width // step
    fetch = [
        pltpu.make_async_copy(virt_hbm, virt_ref, sems.at[0]),
        pltpu.make_async_copy(occ_hbm, occ_ref, sems.at[1]),
    ]
    for part in range(parts):
        span = pl.ds(part * step, step)
        fetch.append(pltpu.make_async_copy(int_hbm.at[:, span], int_ref.at[:, span], sems.at[2 + part]))
    for copy in fetch:
        copy.start()
    va, vb = first_of(va_axes), first_of(vb_axes)
    squeeze = squeezer(step)
    fetch[0].wait()
    fetch[1].wait()
    occ = occ_lanes(occ_ref)
    row_tag = spread(virt_ref, va * row_count, row_count, rows_of((row_count, LANES))) ^ occ_ref[0]
    for part in range(parts):
        fetch[2 + part].wait()
        kept = []
        for block in range(GROUP):
            at = part * GROUP + block
            tag = pair_tags(occ, virt_ref, vb * c_count, at, occ_count)
            held = int_ref[:, at * LANES : (at + 1) * LANES].astype(F32)
            kept.append(jnp.where(row_tag == tag, held, 0.0).astype(BF16))
        small = jnp.dot(jnp.concatenate(kept, 1), squeeze, preferred_element_type=F32)
        small_ref[:, part * LANES : (part + 1) * LANES] = small.astype(BF16)
    peers = out_hbm.shape[0]
    copies = [pltpu.make_async_copy(small_ref, out_hbm.at[peer], sems.at[2 + parts + peer]) for peer in range(peers)]
    for copy in copies:
        copy.start()
    for copy in copies:
        copy.wait()


def squeeze_amp_kernel(va_axes, vb_axes, virt_ref, occ_ref, slab_ref, amp_ref, out_ref):
    row_count, width = amp_ref.shape
    occ_count, slab_count = occ_ref.shape[0], slab_ref.shape[0]
    va, vb = first_of(va_axes), first_of(vb_axes)
    occ = occ_lanes(occ_ref)
    slab = spread(slab_ref, 0, slab_count, rows_of((slab_count, LANES)))
    a_count = row_count // slab_count
    left = jnp.concatenate([slab ^ virt_ref[va * a_count + a] for a in range(a_count)], 0)
    step = GROUP * LANES
    squeeze = squeezer(step)
    for part in range(width // step):
        kept = []
        for block in range(GROUP):
            at = part * GROUP + block
            tag = pair_tags(occ, virt_ref, vb * (width // occ_count), at, occ_count)
            held = amp_ref[:, at * LANES : (at + 1) * LANES].astype(F32)
            kept.append(jnp.where(left == tag, held, 0.0).astype(BF16))
        small = jnp.dot(jnp.concatenate(kept, 1), squeeze, preferred_element_type=F32)
        out_ref[:, part * LANES : (part + 1) * LANES] = small.astype(BF16)


def sort_keys(labels):
    at = lanes(labels.shape)
    return (at // WINDOW) * (WINDOW * GROUP) + labels * WINDOW + at % WINDOW


def column_tags(va_axes, virt_ref, slab_ref, occ_ref, a_count):
    slab_count = slab_ref.shape[0]
    at = lanes((1, a_count * slab_count))
    first = spread(virt_ref, first_of(va_axes) * a_count, a_count, at // slab_count)
    return first ^ spread(slab_ref, 0, slab_count, at % slab_count) ^ occ_ref[0]


def plan_kernel(
    half_rows, va_axes, vb_axes, virt_ref, occ_ref, slab_ref, labels_ref,
    move_ref, tag_ref, columns_ref, place_ref, label_ref, most_ref,
):
    core = lax.axis_index("c")
    columns = column_tags(va_axes, virt_ref, slab_ref, occ_ref, half_rows)
    columns_ref[...] = jnp.broadcast_to(columns, columns_ref.shape)
    labels = labels_ref[...]
    half = lanes(labels.shape) // WINDOW
    most = jnp.int32(0)
    for label in range(GROUP):
        for side in range(LANES // WINDOW):
            hits = jnp.where((labels == label) & (half == side), 1.0, 0.0)
            most = jnp.maximum(most, jnp.max(jnp.sum(hits, axis=1, keepdims=True)).astype(I32))
    most_ref[0] = most

    keys = sort_keys(labels)
    keys_down = jnp.transpose(keys.astype(F32))
    swap = (lanes(keys.shape) // half_rows) % 2 == 0

    def own_first(x):
        x = x.astype(F32)
        swapped = jnp.where(swap, pltpu.roll(x, LANES - half_rows, 1), pltpu.roll(x, half_rows, 1))
        return jnp.where(core == 0, x, swapped)

    keys_across, labels_across = own_first(keys), own_first(labels)
    square = (LANES, LANES)
    for r in range(labels.shape[0]):
        before = jnp.where(keys_down[:, r : r + 1] < keys_across[r : r + 1, :], 1.0, 0.0)
        place = jnp.sum(before, axis=0, keepdims=True)
        moved = jnp.where(rows_of(square).astype(F32) == place, 1.0, 0.0)
        move_ref[r] = moved.astype(BF16)
        tag_ref[r * LANES : (r + 1) * LANES, :] = jnp.broadcast_to(
            jnp.sum(moved * labels_across[r : r + 1, :], axis=1, keepdims=True), square
        ).astype(I32)

    vb, per = first_of(vb_axes), LANES // WINDOW
    row = labels_ref[pl.ds(vb // per, 1), :]
    mine = lanes(row.shape) // WINDOW == vb % per
    key = jnp.where(mine, row * WINDOW + lanes(row.shape) % WINDOW, WINDOW * GROUP).astype(F32)
    own = jnp.where(mine, lanes(row.shape) % WINDOW, -1)
    on_own = rows_of(place_ref.shape) == own
    key_down = jnp.sum(jnp.where(on_own, key, 0.0), axis=1, keepdims=True)
    label_down = jnp.sum(jnp.where(on_own, row.astype(F32), 0.0), axis=1, keepdims=True)
    label_ref[...] = jnp.broadcast_to(label_down, label_ref.shape).astype(I32)
    place = jnp.sum(jnp.where(key < key_down, 1.0, 0.0), axis=1, keepdims=True)
    place_ref[...] = jnp.broadcast_to(place, place_ref.shape).astype(I32)


def multiply_kernel(slots, move_ref, tag_ref, columns_ref, own_ref, other_ref, amp_ref, out_ref, sorted_ref):
    windows = own_ref.shape[0]
    per = LANES // WINDOW
    halves = amp_ref.shape[0] // LANES
    for r in range(windows // per):
        block = jnp.concatenate([x for w in range(r * per, (r + 1) * per) for x in (own_ref[w], other_ref[w])], 0)
        span = slice(r * LANES, (r + 1) * LANES)
        sorted_ref[span, :] = jnp.dot(move_ref[r], block, preferred_element_type=F32).astype(BF16)
    for r in range(windows // per):
        span = slice(r * LANES, (r + 1) * LANES)
        sums = lax.dot_general(
            sorted_ref[span, :], amp_ref[...], (((1,), (1,)), ((), ())), preferred_element_type=F32
        )
        tags = jnp.concatenate([tag_ref[span, :]] * halves, 1)
        sums = jnp.where(tags == columns_ref[0:1, :], sums, 0.0)
        for w in range(per):
            part = sums[w * WINDOW : (w + 1) * WINDOW]
            total = part[:slots]
            for low in range(slots, WINDOW, slots):
                more = part[low : low + slots]
                if more.shape[0] < slots:
                    more = jnp.concatenate([more, jnp.zeros((slots - more.shape[0], more.shape[1]), F32)], 0)
                total = total + more
            largest = jnp.max(jnp.max(jnp.abs(total), axis=0, keepdims=True), axis=1, keepdims=True)
            power = jnp.ceil(jnp.log2(jnp.maximum(largest, SMALLEST)))
            total = total * jnp.exp2(TOP - power)
            code = total * jnp.abs(total)
            square = total * total
            for _ in range(ROOTS - 1):
                code, square = code * square, square * square
            code = code.astype(BF16)
            for half in range(halves):
                out_ref[r * per + w, half * slots : (half + 1) * slots, :] = code[:, half * LANES : (half + 1) * LANES]
            out_ref[r * per + w, halves * slots :, :] = jnp.broadcast_to(power, (GROUP, LANES)).astype(BF16)


def finish_kernel(slots, columns_ref, place_ref, label_ref, parts_ref, out_ref):
    halves = out_ref.shape[1] // LANES
    total = jnp.zeros((halves * slots, LANES), F32)
    for part in range(parts_ref.shape[0]):
        power = parts_ref[part, halves * slots :, :].astype(F32)
        code = parts_ref[part, : halves * slots, :].astype(F32)
        root = jnp.abs(code)
        for _ in range(ROOTS):
            root = jnp.sqrt(root)
        total = total + jnp.where(code < 0.0, -root, root) * jnp.exp2(power[0:1, :] - TOP)
    total = jnp.concatenate([total[half * slots : (half + 1) * slots] for half in range(halves)], 1)
    place = place_ref[:, 0:1]
    slot = jnp.where(place >= 2 * slots, place - 2 * slots, jnp.where(place >= slots, place - slots, place))
    chosen = jnp.where(lanes((WINDOW, slots)) == slot, 1.0, 0.0).astype(BF16)
    full = jnp.dot(chosen, total.astype(BF16), preferred_element_type=F32)
    out_ref[...] = jnp.where(label_ref[...] == columns_ref[0:1, :], full, 0.0).astype(BF16)


def per_device(sizes, amplitudes, integrals, irrep_virt, irrep_occ, irrep_slab):
    va_axes = [(name, sizes[name]) for name in ("xl", "y", "c")]
    vb_axes = [(name, sizes[name]) for name in ("xh", "z")]
    a_rows, slab_count, width = amplitudes.shape
    b_rows = integrals.shape[0]
    depth = width // GROUP
    chips = sizes["xl"] * sizes["y"]
    labels = irrep_virt.reshape(-1, LANES)
    columns = a_rows * slab_count
    shaped = jax.ShapeDtypeStruct

    small = pl.pallas_call(
        functools.partial(squeeze_int_kernel, va_axes, vb_axes),
        out_shape=shaped((chips, b_rows, depth), BF16),
        in_specs=[HBM] * 3,
        out_specs=ANY,
        scratch_shapes=[
            pltpu.SMEM(irrep_virt.shape, I32),
            pltpu.SMEM(irrep_occ.shape, I32),
            pltpu.VMEM((b_rows, width), BF16),
            pltpu.VMEM((b_rows, depth), BF16),
            pltpu.SemaphoreType.DMA((2 + width // (GROUP * LANES) + chips,)),
        ],
        compiler_params=params(),
        name="squeeze_int",
    )(*(pltpu.with_memory_space_constraint(x, pltpu.HBM) for x in (irrep_virt, irrep_occ, integrals)))
    own = lax.all_to_all(small, ("xl", "y"), 0, 0, tiled=False)

    amp_small = pl.pallas_call(
        functools.partial(squeeze_amp_kernel, va_axes, vb_axes),
        out_shape=shaped((columns, depth), BF16),
        in_specs=[SMEM, SMEM, SMEM, VMEM],
        out_specs=VMEM,
        compiler_params=params(),
        cost_estimate=pl.CostEstimate(flops=4 << 30, transcendentals=0, bytes_accessed=8 << 20),
        name="squeeze_amp",
    )(irrep_virt, irrep_occ, irrep_slab, amplitudes.reshape(columns, width))

    *plan, most = pl.pallas_call(
        functools.partial(plan_kernel, b_rows, va_axes, vb_axes),
        out_shape=(
            shaped((labels.shape[0], LANES, LANES), BF16),
            shaped((labels.size, LANES), I32),
            shaped((8, columns), I32),
            shaped((WINDOW, LANES), I32),
            shaped((WINDOW, columns), I32),
            shaped((1,), I32),
        ),
        in_specs=[SMEM, SMEM, SMEM, VMEM],
        out_specs=(VMEM,) * 5 + (SMEM,),
        compiler_params=params(),
        cost_estimate=pl.CostEstimate(flops=2 << 30, transcendentals=0, bytes_accessed=4 << 20),
        name="plan",
    )(irrep_virt, irrep_occ, irrep_slab, labels)

    own, amp_small, most, *plan = lax.optimization_barrier((own, amp_small, most, *plan))
    other = lax.ppermute(own, "c", [(0, 1), (1, 0)])

    def rest(slots, move, tags, column_labels, place, row_labels, own, other, amp_small):
        sent_rows = columns // LANES * slots + GROUP
        parts = pl.pallas_call(
            functools.partial(multiply_kernel, slots),
            out_shape=shaped((chips, sent_rows, LANES), BF16),
            in_specs=[VMEM] * 6,
            out_specs=VMEM,
            scratch_shapes=[pltpu.VMEM((chips * WINDOW, depth), BF16)],
            compiler_params=params(),
            name="multiply",
        )(move, tags, column_labels, own, other, amp_small)
        parts = lax.all_to_all(parts, ("xh", "z"), 0, 0, tiled=False)
        return pl.pallas_call(
            functools.partial(finish_kernel, slots),
            out_shape=shaped((WINDOW, columns), BF16),
            in_specs=[VMEM] * 4,
            out_specs=VMEM,
            compiler_params=params(),
            name="finish",
        )(column_labels, place, row_labels, parts)

    return lax.cond(
        most[0] <= SLOTS,
        functools.partial(rest, SLOTS),
        functools.partial(rest, WINDOW),
        *plan, own, other, amp_small,
    )


def solution(mesh):
    names = ("xl", "y", "c", "xh", "z")
    shape = (2, mesh.shape["va"] // 4, 2, 2, mesh.shape["vb"] // 2)
    fine = Mesh(mesh.devices.reshape(shape), names)
    va, vb = names[:3], names[3:]
    return jax.shard_map(
        functools.partial(per_device, dict(zip(names, shape))),
        mesh=fine,
        in_specs=(P(va, None, vb), P(va, vb), P(), P(), P()),
        out_specs=P(vb, va),
        check_vma=False,
    )
```

```python
import functools

import jax
import jax.numpy as jnp
from jax import lax
from jax.experimental import pallas as pl
from jax.experimental.pallas import tpu as pltpu
from jax.sharding import Mesh, PartitionSpec as P

GROUP = 8
LANES = 128
ROOTS = 4
TOP = 7.0
SMALLEST = 2.0**-100
WINDOW = 64
RUN = 32
SPAN = 16

F32, BF16, I32 = jnp.float32, jnp.bfloat16, jnp.int32
SMEM = pl.BlockSpec(memory_space=pltpu.SMEM)
VMEM = pl.BlockSpec(memory_space=pltpu.VMEM)
HBM = pl.BlockSpec(memory_space=pltpu.HBM)
ANY = pl.BlockSpec(memory_space=pl.ANY)


def params(**more):
    return pltpu.CompilerParams(vmem_limit_bytes=48 << 20, **more)


def lanes(shape):
    return lax.broadcasted_iota(I32, shape, len(shape) - 1)


def rows_of(shape):
    return lax.broadcasted_iota(I32, shape, len(shape) - 2)


def spread(ref, start, count, position):
    out = jnp.zeros_like(position)
    for n in range(count):
        out = jnp.where(position == n, ref[start + n], out)
    return out


def occ_lanes(occ_ref):
    occ_count = occ_ref.shape[0]
    return spread(occ_ref, 0, occ_count, lanes((1, LANES)) % occ_count)


def pair_tags(occ, virt_ref, first_c, block, occ_count):
    per = LANES // occ_count
    c_of = lanes((1, LANES)) // occ_count
    return occ ^ spread(virt_ref, first_c + block * per, per, c_of)


def squeezer(width):
    shape = (width, width // GROUP)
    return jnp.where(rows_of(shape) // GROUP == lanes(shape), 1.0, 0.0).astype(BF16)


def first_of(axis_sizes):
    at = 0
    for name, size in axis_sizes:
        at = at * size + lax.axis_index(name)
    return at


def squeeze_int_kernel(
    va_axes, vb_axes, virt_hbm, occ_hbm, slab_hbm, int_hbm, amp_hbm, out_hbm, amp_ref, pair_ref, left_ref,
    virt_ref, occ_ref, slab_ref, int_ref, small_ref, sems,
):
    row_count, width = int_ref.shape
    occ_count, slab_count = occ_ref.shape[0], slab_ref.shape[0]
    c_count = width // occ_count
    step = GROUP * LANES
    parts = width // step
    fetch = [
        pltpu.make_async_copy(virt_hbm, virt_ref, sems.at[0]),
        pltpu.make_async_copy(occ_hbm, occ_ref, sems.at[1]),
        pltpu.make_async_copy(slab_hbm, slab_ref, sems.at[2]),
    ]
    for part in range(parts):
        span = pl.ds(part * step, step)
        fetch.append(pltpu.make_async_copy(int_hbm.at[:, span], int_ref.at[:, span], sems.at[4 + part]))
    bring = pltpu.make_async_copy(amp_hbm, amp_ref, sems.at[3])
    for copy in fetch:
        copy.start()
    bring.start()
    va, vb = first_of(va_axes), first_of(vb_axes)
    squeeze = squeezer(step)
    for copy in fetch[:3]:
        copy.wait()
    occ = occ_lanes(occ_ref)
    row_tag = spread(virt_ref, va * row_count, row_count, rows_of((row_count, LANES))) ^ occ_ref[0]
    for part in range(parts):
        fetch[3 + part].wait()
        kept = []
        for block in range(GROUP):
            at = part * GROUP + block
            tag = pair_tags(occ, virt_ref, vb * c_count, at, occ_count)
            pair_ref[at : at + 1, :] = tag
            held = int_ref[:, at * LANES : (at + 1) * LANES].astype(F32)
            kept.append(jnp.where(row_tag == tag, held, 0.0).astype(BF16))
        small = jnp.dot(jnp.concatenate(kept, 1), squeeze, preferred_element_type=F32)
        small_ref[:, part * LANES : (part + 1) * LANES] = small.astype(BF16)
    peers, share = out_hbm.shape[0], out_hbm.shape[1]
    copies = []
    for peer in range(peers):
        part = peer // (peers * share // row_count)
        rows = small_ref.at[part * share : (part + 1) * share]
        copies.append(pltpu.make_async_copy(rows, out_hbm.at[peer], sems.at[4 + parts + peer]))
    for copy in copies:
        copy.start()
    slab = spread(slab_ref, 0, slab_count, rows_of((slab_count, LANES)))
    for a in range(row_count):
        left_ref[a * slab_count : (a + 1) * slab_count, :] = slab ^ virt_ref[va * row_count + a]
    for copy in copies:
        copy.wait()
    bring.wait()


def squeeze_amp_kernel(pair_ref, left_ref, amp_ref, out_ref):
    width = amp_ref.shape[1]
    left = left_ref[...]
    step = GROUP * LANES
    squeeze = squeezer(step)
    for part in range(width // step):
        kept = []
        for block in range(GROUP):
            at = part * GROUP + block
            held = amp_ref[:, at * LANES : (at + 1) * LANES].astype(F32)
            kept.append(jnp.where(left == pair_ref[at : at + 1, :], held, 0.0).astype(BF16))
        small = jnp.dot(jnp.concatenate(kept, 1), squeeze, preferred_element_type=F32)
        out_ref[:, part * LANES : (part + 1) * LANES] = small.astype(BF16)


def sort_keys(labels):
    at = lanes(labels.shape)
    return (at // RUN) * (RUN * GROUP) + labels * RUN + at % RUN


def column_tags(va, virt_ref, slab_ref, occ_ref, a_count):
    slab_count = slab_ref.shape[0]
    at = lanes((1, a_count * slab_count))
    first = spread(virt_ref, va * a_count, a_count, at // slab_count)
    return first ^ spread(slab_ref, 0, slab_count, at % slab_count) ^ occ_ref[0]


def plan_kernel(
    a_count, va_axes, vb_axes, virt_ref, occ_ref, slab_ref, labels_ref,
    move_ref, tag_ref, columns_ref, place_ref, label_ref, most_ref,
):
    core, share = lax.axis_index("c"), lax.axis_index("xl")
    va, vb = first_of(va_axes), first_of(vb_axes)
    across = va_axes[1][1] * va_axes[2][1]
    partner = va + (1 - 2 * share) * across
    for side, at in enumerate((va, partner)):
        tags = column_tags(at, virt_ref, slab_ref, occ_ref, a_count)
        columns_ref[8 * side : 8 * side + 8, :] = jnp.broadcast_to(tags, (8, tags.shape[1]))
    labels = labels_ref[...]
    run = lanes(labels.shape) // RUN
    most = jnp.int32(0)
    for label in range(GROUP):
        for side in range(LANES // RUN):
            hits = jnp.where((labels == label) & (run == side), 1.0, 0.0)
            most = jnp.maximum(most, jnp.max(jnp.sum(hits, axis=1, keepdims=True)).astype(I32))
    most_ref[0] = most

    count = labels.shape[0] // 2
    mine = jnp.where(share == 0, labels[:count], labels[count:])
    mine = jnp.concatenate([mine, mine], 0)
    keys = sort_keys(mine)
    keys_down = jnp.transpose(keys.astype(F32))
    half = RUN // 2
    swap = (lanes(keys.shape) // half) % 2 == 0

    def own_first(x):
        x = x.astype(F32)
        swapped = jnp.where(swap, pltpu.roll(x, LANES - half, 1), pltpu.roll(x, half, 1))
        return jnp.where(core == 0, x, swapped)

    keys_across, labels_across = own_first(keys), own_first(mine)
    square = (LANES, LANES)
    for r in range(count):
        before = jnp.where(keys_down[:, r : r + 1] < keys_across[r : r + 1, :], 1.0, 0.0)
        place = jnp.sum(before, axis=0, keepdims=True)
        moved = jnp.where(rows_of(square).astype(F32) == place, 1.0, 0.0)
        move_ref[r] = moved.astype(BF16)
        tag_ref[r * LANES : (r + 1) * LANES, :] = jnp.broadcast_to(
            jnp.sum(moved * labels_across[r : r + 1, :], axis=1, keepdims=True), square
        ).astype(I32)

    per = LANES // RUN
    for part in range(2):
        row = labels_ref[pl.ds(part * count + vb // per, 1), :]
        held = lanes(row.shape) // RUN == vb % per
        key = jnp.where(held, row * RUN + lanes(row.shape) % RUN, RUN * GROUP).astype(F32)
        on_own = rows_of((RUN, LANES)) == jnp.where(held, lanes(row.shape) % RUN, -1)
        key_down = jnp.sum(jnp.where(on_own, key, 0.0), axis=1, keepdims=True)
        label_down = jnp.sum(jnp.where(on_own, row.astype(F32), 0.0), axis=1, keepdims=True)
        place = jnp.sum(jnp.where(key < key_down, 1.0, 0.0), axis=1, keepdims=True)
        place_ref[part * RUN : (part + 1) * RUN, :] = jnp.broadcast_to(place, (RUN, LANES)).astype(I32)
        label_ref[part * RUN : (part + 1) * RUN, :] = jnp.broadcast_to(label_down, (RUN, label_ref.shape[1])).astype(I32)


def folded(part, span):
    count = part.shape[0]
    if span > count:
        return jnp.concatenate([part, jnp.zeros((span - count, part.shape[1]), F32)], 0)
    slots = span - 1
    row = rows_of((span, part.shape[1]))
    total = jnp.where(row < slots, part[:span], 0.0)
    for low in range(slots, count, slots):
        moved = pltpu.roll(part, count - low, 0)[:span]
        total = total + jnp.where(row < min(slots, count - low), moved, 0.0)
    return total


def multiply_kernel(span, move_ref, tag_ref, columns_ref, own_ref, other_ref, amp_ref, partner_ref, out_ref, sorted_ref):
    windows = own_ref.shape[0]
    per = LANES // RUN
    halves = amp_ref.shape[0] // LANES
    share = lax.axis_index("xl")
    for r in range(windows // per):
        block = jnp.concatenate([x for w in range(r * per, (r + 1) * per) for x in (own_ref[w], other_ref[w])], 0)
        sorted_ref[r * LANES : (r + 1) * LANES, :] = jnp.dot(
            move_ref[r], block, preferred_element_type=F32
        ).astype(BF16)
    for side, columns_of in enumerate((amp_ref, partner_ref)):
        first = (share if side == 0 else 1 - share) * windows
        for r in range(windows // per):
            at = slice(r * LANES, (r + 1) * LANES)
            sums = lax.dot_general(
                sorted_ref[at, :], columns_of[...], (((1,), (1,)), ((), ())), preferred_element_type=F32
            )
            tags = jnp.concatenate([tag_ref[at, :]] * halves, 1)
            sums = jnp.where(tags == columns_ref[8 * side : 8 * side + 1, :], sums, 0.0)
            for w in range(per):
                total = folded(sums[w * RUN : (w + 1) * RUN], span)
                largest = jnp.max(jnp.max(jnp.abs(total), axis=0, keepdims=True), axis=1, keepdims=True)
                power = jnp.ceil(jnp.log2(jnp.maximum(largest, SMALLEST)))
                total = total * jnp.exp2(TOP - power)
                code = total * jnp.abs(total)
                square = total * total
                for _ in range(ROOTS - 1):
                    code, square = code * square, square * square
                code = jnp.where(rows_of(code.shape) == span - 1, power, code).astype(BF16)
                for half in range(halves):
                    out_ref[first + r * per + w, half * span : (half + 1) * span, :] = code[:, half * LANES : (half + 1) * LANES]


def finish_kernel(span, columns_ref, place_ref, label_ref, parts_ref, out_ref):
    halves = out_ref.shape[1] // LANES
    sources = parts_ref.shape[0] // 2
    slots = span - 1
    for part in range(2):
        totals = []
        for half in range(halves):
            total = jnp.zeros((span, LANES), F32)
            for source in range(sources):
                code = parts_ref[part * sources + source, half * span : (half + 1) * span, :].astype(F32)
                root = jnp.abs(code)
                for _ in range(ROOTS):
                    root = jnp.sqrt(root)
                total = total + jnp.where(code < 0.0, -root, root) * jnp.exp2(code[span - 1 :, :] - TOP)
            totals.append(total)
        at = slice(part * RUN, (part + 1) * RUN)
        place = place_ref[at, 0:1]
        slot = jnp.where(place >= 2 * slots, place - 2 * slots, jnp.where(place >= slots, place - slots, place))
        chosen = jnp.where(lanes((RUN, span)) == slot, 1.0, 0.0).astype(BF16)
        full = jnp.dot(chosen, jnp.concatenate(totals, 1).astype(BF16), preferred_element_type=F32)
        full = jnp.where(label_ref[at, :] == columns_ref[0:1, :], full, 0.0).astype(BF16)
        half_run = RUN // 2
        for core in range(2):
            low = core * RUN + part * half_run
            out_ref[low : low + half_run, :] = full[core * half_run : (core + 1) * half_run]


def per_device(sizes, amplitudes, integrals, irrep_virt, irrep_occ, irrep_slab):
    va_axes = [(name, sizes[name]) for name in ("xl", "y", "c")]
    vb_axes = [(name, sizes[name]) for name in ("xh", "z")]
    a_rows, slab_count, width = amplitudes.shape
    b_rows = integrals.shape[0]
    depth = width // GROUP
    chips = sizes["xl"] * sizes["y"]
    columns = a_rows * slab_count
    shaped = jax.ShapeDtypeStruct
    share = b_rows // sizes["xl"]

    arrays = (irrep_virt, irrep_occ, irrep_slab, integrals, amplitudes.reshape(columns, width))
    small, amp_near, pair_tag, left_tag = pl.pallas_call(
        functools.partial(squeeze_int_kernel, va_axes, vb_axes),
        out_shape=(
            shaped((chips, share, depth), BF16),
            shaped((columns, width), BF16),
            shaped((width // LANES, LANES), I32),
            shaped((columns, LANES), I32),
        ),
        in_specs=[HBM] * 5,
        out_specs=(ANY, VMEM, VMEM, VMEM),
        scratch_shapes=[
            pltpu.SMEM(irrep_virt.shape, I32),
            pltpu.SMEM(irrep_occ.shape, I32),
            pltpu.SMEM(irrep_slab.shape, I32),
            pltpu.VMEM((b_rows, width), BF16),
            pltpu.VMEM((b_rows, depth), BF16),
            pltpu.SemaphoreType.DMA((4 + width // (GROUP * LANES) + chips,)),
        ],
        compiler_params=params(),
        name="squeeze_int",
    )(*(pltpu.with_memory_space_constraint(x, pltpu.HBM) for x in arrays))
    own = lax.all_to_all(small, ("xl", "y"), 0, 0, tiled=False)

    amp_small = pl.pallas_call(
        squeeze_amp_kernel,
        out_shape=shaped((columns, depth), BF16),
        in_specs=[VMEM] * 3,
        out_specs=VMEM,
        compiler_params=params(),
        cost_estimate=pl.CostEstimate(flops=4 << 30, transcendentals=0, bytes_accessed=8 << 20),
        name="squeeze_amp",
    )(pair_tag, left_tag, amp_near)
    amp_partner = lax.ppermute(amp_small, "xl", [(0, 1), (1, 0)])

    labels = irrep_virt.reshape(chips, sizes["c"], sizes["xl"], share).transpose(2, 0, 1, 3).reshape(-1, LANES)
    *plan, most = pl.pallas_call(
        functools.partial(plan_kernel, a_rows, va_axes, vb_axes),
        out_shape=(
            shaped((labels.shape[0] // 2, LANES, LANES), BF16),
            shaped((labels.size // 2, LANES), I32),
            shaped((16, columns), I32),
            shaped((WINDOW, LANES), I32),
            shaped((WINDOW, columns), I32),
            shaped((1,), I32),
        ),
        in_specs=[SMEM, SMEM, SMEM, VMEM],
        out_specs=(VMEM,) * 5 + (SMEM,),
        compiler_params=params(),
        cost_estimate=pl.CostEstimate(flops=2 << 30, transcendentals=0, bytes_accessed=4 << 20),
        name="plan",
    )(irrep_virt, irrep_occ, irrep_slab, labels)

    def rest(span, move, tags, column_labels, place, row_labels, own, other, amp_small, amp_partner):
        parts = pl.pallas_call(
            functools.partial(multiply_kernel, span),
            out_shape=shaped((2 * chips, columns // LANES * span, LANES), BF16),
            in_specs=[VMEM] * 7,
            out_specs=VMEM,
            scratch_shapes=[pltpu.VMEM((chips * RUN, depth), BF16)],
            compiler_params=params(),
            name="multiply",
        )(move, tags, column_labels, own, other, amp_small, amp_partner)
        parts = lax.all_to_all(parts, ("xl", "xh", "z"), 0, 0, tiled=False)
        return pl.pallas_call(
            functools.partial(finish_kernel, span),
            out_shape=shaped((WINDOW, columns), BF16),
            in_specs=[VMEM] * 4,
            out_specs=VMEM,
            compiler_params=params(),
            name="finish",
        )(column_labels, place, row_labels, parts)

    own, amp_small, most, *plan = lax.optimization_barrier((own, amp_small, most, *plan))
    other = lax.ppermute(own, "c", [(0, 1), (1, 0)])

    return lax.cond(
        most[0] < SPAN,
        functools.partial(rest, SPAN),
        functools.partial(rest, RUN + 8),
        *plan, own, other, amp_small, amp_partner,
    )


def solution(mesh):
    names = ("xl", "y", "c", "xh", "z")
    shape = (2, mesh.shape["va"] // 4, 2, 2, mesh.shape["vb"] // 2)
    fine = Mesh(mesh.devices.reshape(shape), names)
    va, vb = names[:3], names[3:]
    return jax.shard_map(
        functools.partial(per_device, dict(zip(names, shape))),
        mesh=fine,
        in_specs=(P(va, None, vb), P(va, vb), P(), P(), P()),
        out_specs=P(vb, va),
        check_vma=False,
    )
```

```python
import functools

import jax
import jax.numpy as jnp
from jax import lax
from jax.experimental import pallas as pl
from jax.experimental.pallas import tpu as pltpu
from jax.sharding import Mesh, PartitionSpec as P

GROUP = 8
LANES = 128
ROOTS = 4
TOP = 7.0
SMALLEST = 2.0**-100
WINDOW = 64
RUN = 32
SPANS = (12, 16)

F32, BF16, I32 = jnp.float32, jnp.bfloat16, jnp.int32
SMEM = pl.BlockSpec(memory_space=pltpu.SMEM)
VMEM = pl.BlockSpec(memory_space=pltpu.VMEM)
HBM = pl.BlockSpec(memory_space=pltpu.HBM)
ANY = pl.BlockSpec(memory_space=pl.ANY)


def params(**more):
    return pltpu.CompilerParams(vmem_limit_bytes=48 << 20, **more)


def lanes(shape):
    return lax.broadcasted_iota(I32, shape, len(shape) - 1)


def rows_of(shape):
    return lax.broadcasted_iota(I32, shape, len(shape) - 2)


def spread(ref, start, count, position):
    out = jnp.zeros_like(position)
    for n in range(count):
        out = jnp.where(position == n, ref[start + n], out)
    return out


def occ_lanes(occ_ref):
    occ_count = occ_ref.shape[0]
    return spread(occ_ref, 0, occ_count, lanes((1, LANES)) % occ_count)


def pair_tags(occ, virt_ref, first_c, block, occ_count):
    per = LANES // occ_count
    c_of = lanes((1, LANES)) // occ_count
    return occ ^ spread(virt_ref, first_c + block * per, per, c_of)


def squeezer(width):
    shape = (width, width // GROUP)
    return jnp.where(rows_of(shape) // GROUP == lanes(shape), 1.0, 0.0).astype(BF16)


def first_of(axis_sizes):
    at = 0
    for name, size in axis_sizes:
        at = at * size + lax.axis_index(name)
    return at


def squeeze_int_kernel(
    va_axes, vb_axes, virt_hbm, occ_hbm, slab_hbm, int_hbm, amp_hbm, out_hbm, amp_ref, pair_ref, left_ref,
    virt_ref, occ_ref, slab_ref, int_ref, small_ref, sems,
):
    row_count, width = int_ref.shape
    occ_count, slab_count = occ_ref.shape[0], slab_ref.shape[0]
    c_count = width // occ_count
    step = GROUP * LANES
    parts = width // step
    fetch = [
        pltpu.make_async_copy(virt_hbm, virt_ref, sems.at[0]),
        pltpu.make_async_copy(occ_hbm, occ_ref, sems.at[1]),
        pltpu.make_async_copy(slab_hbm, slab_ref, sems.at[2]),
    ]
    for part in range(parts):
        span = pl.ds(part * step, step)
        fetch.append(pltpu.make_async_copy(int_hbm.at[:, span], int_ref.at[:, span], sems.at[4 + part]))
    bring = pltpu.make_async_copy(amp_hbm, amp_ref, sems.at[3])
    for copy in fetch:
        copy.start()
    bring.start()
    va, vb = first_of(va_axes), first_of(vb_axes)
    squeeze = squeezer(step)
    for copy in fetch[:3]:
        copy.wait()
    occ = occ_lanes(occ_ref)
    row_tag = spread(virt_ref, va * row_count, row_count, rows_of((row_count, LANES))) ^ occ_ref[0]
    stacked = []
    for part in range(parts):
        fetch[3 + part].wait()
        kept = []
        for block in range(GROUP):
            at = part * GROUP + block
            tag = pair_tags(occ, virt_ref, vb * c_count, at, occ_count)
            pair_ref[at : at + 1, :] = tag
            held = int_ref[:, at * LANES : (at + 1) * LANES].astype(F32)
            kept.append(jnp.where(row_tag == tag, held, 0.0).astype(BF16))
        stacked.append(jnp.concatenate(kept, 1))
    small = jnp.dot(jnp.concatenate(stacked, 0), squeeze, preferred_element_type=F32).astype(BF16)
    for part in range(parts):
        small_ref[:, part * LANES : (part + 1) * LANES] = small[part * row_count : (part + 1) * row_count]
    peers, share = out_hbm.shape[0], out_hbm.shape[1]
    copies = []
    for peer in range(peers):
        part = peer // (peers * share // row_count)
        rows = small_ref.at[part * share : (part + 1) * share]
        copies.append(pltpu.make_async_copy(rows, out_hbm.at[peer], sems.at[4 + parts + peer]))
    for copy in copies:
        copy.start()
    slab = spread(slab_ref, 0, slab_count, rows_of((slab_count, LANES)))
    for a in range(row_count):
        left_ref[a * slab_count : (a + 1) * slab_count, :] = slab ^ virt_ref[va * row_count + a]
    for copy in copies:
        copy.wait()
    bring.wait()


def squeeze_amp_kernel(pair_ref, left_ref, amp_ref, out_ref):
    width = amp_ref.shape[1]
    left = left_ref[...]
    step = GROUP * LANES
    squeeze = squeezer(step)
    for part in range(width // step):
        kept = []
        for block in range(GROUP):
            at = part * GROUP + block
            held = amp_ref[:, at * LANES : (at + 1) * LANES].astype(F32)
            kept.append(jnp.where(left == pair_ref[at : at + 1, :], held, 0.0).astype(BF16))
        small = jnp.dot(jnp.concatenate(kept, 1), squeeze, preferred_element_type=F32)
        out_ref[:, part * LANES : (part + 1) * LANES] = small.astype(BF16)


def sort_keys(labels):
    at = lanes(labels.shape)
    return (at // RUN) * (RUN * GROUP) + labels * RUN + at % RUN


def column_tags(va, virt_ref, slab_ref, occ_ref, a_count):
    slab_count = slab_ref.shape[0]
    at = lanes((1, a_count * slab_count))
    first = spread(virt_ref, va * a_count, a_count, at // slab_count)
    return first ^ spread(slab_ref, 0, slab_count, at % slab_count) ^ occ_ref[0]


def plan_kernel(
    a_count, va_axes, vb_axes, virt_ref, occ_ref, slab_ref, labels_ref,
    move_ref, tag_ref, columns_ref, place_ref, label_ref, most_ref,
):
    share = lax.axis_index("xl")
    va, vb = first_of(va_axes), first_of(vb_axes)
    across = va_axes[1][1] * va_axes[2][1]
    partner = va + (1 - 2 * share) * across
    for side, at in enumerate((va, partner)):
        tags = column_tags(at, virt_ref, slab_ref, occ_ref, a_count)
        columns_ref[8 * side : 8 * side + 8, :] = jnp.broadcast_to(tags, (8, tags.shape[1]))
    labels = labels_ref[...]
    run = lanes(labels.shape) // RUN
    most = jnp.int32(0)
    for label in range(GROUP):
        for side in range(LANES // RUN):
            hits = jnp.where((labels == label) & (run == side), 1.0, 0.0)
            most = jnp.maximum(most, jnp.max(jnp.sum(hits, axis=1, keepdims=True)).astype(I32))
    most_ref[0] = most

    count = labels.shape[0] // 2
    mine = jnp.where(share == 0, labels[:count], labels[count:])
    mine = jnp.concatenate([mine, mine], 0)
    keys_across, labels_across = sort_keys(mine).astype(F32), mine.astype(F32)
    keys_down = jnp.transpose(keys_across)
    square = (LANES, LANES)
    for r in range(count):
        before = jnp.where(keys_down[:, r : r + 1] < keys_across[r : r + 1, :], 1.0, 0.0)
        place = jnp.sum(before, axis=0, keepdims=True)
        moved = jnp.where(rows_of(square).astype(F32) == place, 1.0, 0.0)
        move_ref[r] = moved.astype(BF16)
        tag_ref[r * LANES : (r + 1) * LANES, :] = jnp.broadcast_to(
            jnp.sum(moved * labels_across[r : r + 1, :], axis=1, keepdims=True), square
        ).astype(I32)

    per = LANES // RUN
    for part in range(2):
        row = labels_ref[pl.ds(part * count + vb // per, 1), :]
        held = lanes(row.shape) // RUN == vb % per
        key = jnp.where(held, row * RUN + lanes(row.shape) % RUN, RUN * GROUP).astype(F32)
        on_own = rows_of((RUN, LANES)) == jnp.where(held, lanes(row.shape) % RUN, -1)
        key_down = jnp.sum(jnp.where(on_own, key, 0.0), axis=1, keepdims=True)
        label_down = jnp.sum(jnp.where(on_own, row.astype(F32), 0.0), axis=1, keepdims=True)
        place = jnp.sum(jnp.where(key < key_down, 1.0, 0.0), axis=1, keepdims=True)
        place_ref[part * RUN : (part + 1) * RUN, :] = jnp.broadcast_to(place, (RUN, LANES)).astype(I32)
        label_ref[part * RUN : (part + 1) * RUN, :] = jnp.broadcast_to(label_down, (RUN, label_ref.shape[1])).astype(I32)


def folded(part, span):
    count = part.shape[0]
    if span > count:
        return jnp.concatenate([part, jnp.zeros((span - count, part.shape[1]), F32)], 0)
    slots = span - 1
    row = rows_of((span, part.shape[1]))
    total = jnp.where(row < slots, part[:span], 0.0)
    for low in range(slots, count, slots):
        moved = pltpu.roll(part, count - low, 0)[:span]
        total = total + jnp.where(row < min(slots, count - low), moved, 0.0)
    return total


def multiply_kernel(span, move_ref, tag_ref, columns_ref, rows_ref, amp_ref, partner_ref, out_ref, sorted_ref):
    cores, windows = rows_ref.shape[:2]
    per = LANES // RUN
    halves = amp_ref.shape[0] // LANES
    share = lax.axis_index("xl")
    for r in range(windows // per):
        block = jnp.concatenate([x for w in range(r * per, (r + 1) * per) for x in [rows_ref[core, w] for core in range(cores)]], 0)
        sorted_ref[r * LANES : (r + 1) * LANES, :] = jnp.dot(
            move_ref[r], block, preferred_element_type=F32
        ).astype(BF16)
    for side, columns_of in enumerate((amp_ref, partner_ref)):
        first = (share if side == 0 else 1 - share) * windows
        for r in range(windows // per):
            at = slice(r * LANES, (r + 1) * LANES)
            sums = lax.dot_general(
                sorted_ref[at, :], columns_of[...], (((1,), (1,)), ((), ())), preferred_element_type=F32
            )
            tags = jnp.concatenate([tag_ref[at, :]] * halves, 1)
            sums = jnp.where(tags == columns_ref[8 * side : 8 * side + 1, :], sums, 0.0)
            for w in range(per):
                total = folded(sums[w * RUN : (w + 1) * RUN], span)
                largest = jnp.max(jnp.max(jnp.abs(total), axis=0, keepdims=True), axis=1, keepdims=True)
                power = jnp.ceil(jnp.log2(jnp.maximum(largest, SMALLEST)))
                total = total * jnp.exp2(TOP - power)
                code = total * jnp.abs(total)
                square = total * total
                for _ in range(ROOTS - 1):
                    code, square = code * square, square * square
                code = jnp.where(rows_of(code.shape) == span - 1, power, code).astype(BF16)
                for half in range(halves):
                    out_ref[first + r * per + w, half * span : (half + 1) * span, :] = code[:, half * LANES : (half + 1) * LANES]


def finish_kernel(span, columns_ref, place_ref, label_ref, parts_ref, out_ref):
    halves = out_ref.shape[1] // LANES
    sources = parts_ref.shape[0] // 2
    slots = span - 1
    for part in range(2):
        totals = []
        for half in range(halves):
            total = jnp.zeros((span, LANES), F32)
            for source in range(sources):
                code = parts_ref[part * sources + source, half * span : (half + 1) * span, :].astype(F32)
                root = jnp.abs(code)
                for _ in range(ROOTS):
                    root = jnp.sqrt(root)
                total = total + jnp.where(code < 0.0, -root, root) * jnp.exp2(code[span - 1 :, :] - TOP)
            totals.append(total)
        at = slice(part * RUN, (part + 1) * RUN)
        place = place_ref[at, 0:1]
        slot = jnp.where(place >= 2 * slots, place - 2 * slots, jnp.where(place >= slots, place - slots, place))
        chosen = jnp.where(lanes((RUN, span)) == slot, 1.0, 0.0).astype(BF16)
        full = jnp.dot(chosen, jnp.concatenate(totals, 1).astype(BF16), preferred_element_type=F32)
        full = jnp.where(label_ref[at, :] == columns_ref[0:1, :], full, 0.0).astype(BF16)
        half_run = RUN // 2
        for core in range(2):
            low = core * RUN + part * half_run
            out_ref[low : low + half_run, :] = full[core * half_run : (core + 1) * half_run]


def per_device(sizes, amplitudes, integrals, irrep_virt, irrep_occ, irrep_slab):
    va_axes = [(name, sizes[name]) for name in ("xl", "y", "c")]
    vb_axes = [(name, sizes[name]) for name in ("xh", "z")]
    a_rows, slab_count, width = amplitudes.shape
    b_rows = integrals.shape[0]
    depth = width // GROUP
    chips = sizes["xl"] * sizes["y"]
    columns = a_rows * slab_count
    shaped = jax.ShapeDtypeStruct
    share = b_rows // sizes["xl"]

    arrays = (irrep_virt, irrep_occ, irrep_slab, integrals, amplitudes.reshape(columns, width))
    small, amp_near, pair_tag, left_tag = pl.pallas_call(
        functools.partial(squeeze_int_kernel, va_axes, vb_axes),
        out_shape=(
            shaped((chips, share, depth), BF16),
            shaped((columns, width), BF16),
            shaped((width // LANES, LANES), I32),
            shaped((columns, LANES), I32),
        ),
        in_specs=[HBM] * 5,
        out_specs=(ANY, VMEM, VMEM, VMEM),
        scratch_shapes=[
            pltpu.SMEM(irrep_virt.shape, I32),
            pltpu.SMEM(irrep_occ.shape, I32),
            pltpu.SMEM(irrep_slab.shape, I32),
            pltpu.VMEM((b_rows, width), BF16),
            pltpu.VMEM((b_rows, depth), BF16),
            pltpu.SemaphoreType.DMA((4 + width // (GROUP * LANES) + chips,)),
        ],
        compiler_params=params(),
        name="squeeze_int",
    )(*(pltpu.with_memory_space_constraint(x, pltpu.HBM) for x in arrays))
    own = lax.all_to_all(small, ("xl", "y"), 0, 0, tiled=False)

    amp_small = pl.pallas_call(
        squeeze_amp_kernel,
        out_shape=shaped((columns, depth), BF16),
        in_specs=[VMEM] * 3,
        out_specs=VMEM,
        compiler_params=params(),
        cost_estimate=pl.CostEstimate(flops=4 << 30, transcendentals=0, bytes_accessed=8 << 20),
        name="squeeze_amp",
    )(pair_tag, left_tag, amp_near)
    amp_partner = lax.ppermute(amp_small, "xl", [(0, 1), (1, 0)])

    labels = irrep_virt.reshape(chips, sizes["c"], sizes["xl"], share).transpose(2, 0, 1, 3).reshape(-1, LANES)
    *plan, most = pl.pallas_call(
        functools.partial(plan_kernel, a_rows, va_axes, vb_axes),
        out_shape=(
            shaped((labels.shape[0] // 2, LANES, LANES), BF16),
            shaped((labels.size // 2, LANES), I32),
            shaped((16, columns), I32),
            shaped((WINDOW, LANES), I32),
            shaped((WINDOW, columns), I32),
            shaped((1,), I32),
        ),
        in_specs=[SMEM, SMEM, SMEM, VMEM],
        out_specs=(VMEM,) * 5 + (SMEM,),
        compiler_params=params(),
        cost_estimate=pl.CostEstimate(flops=2 << 30, transcendentals=0, bytes_accessed=4 << 20),
        name="plan",
    )(irrep_virt, irrep_occ, irrep_slab, labels)

    def rest(span, move, tags, column_labels, place, row_labels, both, amp_small, amp_partner):
        parts = pl.pallas_call(
            functools.partial(multiply_kernel, span),
            out_shape=shaped((2 * chips, columns // LANES * span, LANES), BF16),
            in_specs=[VMEM] * 6,
            out_specs=VMEM,
            scratch_shapes=[pltpu.VMEM((chips * RUN, depth), BF16)],
            compiler_params=params(),
            name="multiply",
        )(move, tags, column_labels, both, amp_small, amp_partner)
        parts = lax.all_to_all(parts, ("xl", "xh", "z"), 0, 0, tiled=False)
        return pl.pallas_call(
            functools.partial(finish_kernel, span),
            out_shape=shaped((WINDOW, columns), BF16),
            in_specs=[VMEM] * 4,
            out_specs=VMEM,
            compiler_params=params(),
            name="finish",
        )(column_labels, place, row_labels, parts)

    own, amp_small, most, *plan = lax.optimization_barrier((own, amp_small, most, *plan))
    both = lax.all_gather(own, "c", axis=0, tiled=False)

    return lax.switch(
        sum((most[0] >= span).astype(I32) for span in SPANS),
        [functools.partial(rest, span) for span in (*SPANS, RUN + 8)],
        *plan, both, amp_small, amp_partner,
    )


def solution(mesh):
    names = ("xl", "y", "c", "xh", "z")
    shape = (2, mesh.shape["va"] // 4, 2, 2, mesh.shape["vb"] // 2)
    fine = Mesh(mesh.devices.reshape(shape), names)
    va, vb = names[:3], names[3:]
    return jax.shard_map(
        functools.partial(per_device, dict(zip(names, shape))),
        mesh=fine,
        in_specs=(P(va, None, vb), P(va, vb), P(), P(), P()),
        out_specs=P(vb, va),
        check_vma=False,
    )
```

```python
import functools

import jax
import jax.numpy as jnp
from jax import lax
from jax.experimental import pallas as pl
from jax.experimental.pallas import tpu as pltpu
from jax.sharding import Mesh, PartitionSpec as P

GROUP = 8
LANES = 128
ROOTS = 4
TOP = 7.0
SMALLEST = 2.0**-100
WINDOW = 64
RUN = 32
SPANS = (12, 16)

F32, BF16, I32 = jnp.float32, jnp.bfloat16, jnp.int32
SMEM = pl.BlockSpec(memory_space=pltpu.SMEM)
VMEM = pl.BlockSpec(memory_space=pltpu.VMEM)
HBM = pl.BlockSpec(memory_space=pltpu.HBM)
ANY = pl.BlockSpec(memory_space=pl.ANY)


def params(**more):
    return pltpu.CompilerParams(vmem_limit_bytes=48 << 20, **more)


def lanes(shape):
    return lax.broadcasted_iota(I32, shape, len(shape) - 1)


def rows_of(shape):
    return lax.broadcasted_iota(I32, shape, len(shape) - 2)


def spread(ref, start, count, position):
    out = jnp.zeros_like(position)
    for n in range(count):
        out = jnp.where(position == n, ref[start + n], out)
    return out


def occ_lanes(occ_ref):
    occ_count = occ_ref.shape[0]
    return spread(occ_ref, 0, occ_count, lanes((1, LANES)) % occ_count)


def pair_tags(occ, virt_ref, first_c, block, occ_count):
    per = LANES // occ_count
    c_of = lanes((1, LANES)) // occ_count
    return occ ^ spread(virt_ref, first_c + block * per, per, c_of)


def squeezer(width):
    shape = (width, width // GROUP)
    return jnp.where(rows_of(shape) // GROUP == lanes(shape), 1.0, 0.0).astype(BF16)


def first_of(axis_sizes):
    at = 0
    for name, size in axis_sizes:
        at = at * size + lax.axis_index(name)
    return at


def squeeze_int_kernel(
    va_axes, vb_axes, virt_hbm, occ_hbm, slab_hbm, int_hbm, amp_hbm, out_hbm, amp_ref, pair_ref, left_ref,
    virt_ref, occ_ref, slab_ref, int_ref, small_ref, sems,
):
    row_count, width = int_ref.shape
    occ_count, slab_count = occ_ref.shape[0], slab_ref.shape[0]
    c_count = width // occ_count
    step = GROUP * LANES
    parts = width // step
    fetch = [
        pltpu.make_async_copy(virt_hbm, virt_ref, sems.at[0]),
        pltpu.make_async_copy(occ_hbm, occ_ref, sems.at[1]),
        pltpu.make_async_copy(slab_hbm, slab_ref, sems.at[2]),
    ]
    for part in range(parts):
        span = pl.ds(part * step, step)
        fetch.append(pltpu.make_async_copy(int_hbm.at[:, span], int_ref.at[:, span], sems.at[4 + part]))
    bring = pltpu.make_async_copy(amp_hbm, amp_ref, sems.at[3])
    for copy in fetch:
        copy.start()
    bring.start()
    va, vb = first_of(va_axes), first_of(vb_axes)
    squeeze = squeezer(step)
    for copy in fetch[:3]:
        copy.wait()
    occ = occ_lanes(occ_ref)
    row_tag = spread(virt_ref, va * row_count, row_count, rows_of((row_count, LANES))) ^ occ_ref[0]
    stacked = []
    for part in range(parts):
        fetch[3 + part].wait()
        kept = []
        for block in range(GROUP):
            at = part * GROUP + block
            tag = pair_tags(occ, virt_ref, vb * c_count, at, occ_count)
            pair_ref[at : at + 1, :] = tag
            held = int_ref[:, at * LANES : (at + 1) * LANES].astype(F32)
            kept.append(jnp.where(row_tag == tag, held, 0.0).astype(BF16))
        stacked.append(jnp.concatenate(kept, 1))
    small = jnp.dot(jnp.concatenate(stacked, 0), squeeze, preferred_element_type=F32).astype(BF16)
    for part in range(parts):
        small_ref[:, part * LANES : (part + 1) * LANES] = small[part * row_count : (part + 1) * row_count]
    peers, share = out_hbm.shape[0], out_hbm.shape[1]
    copies = []
    for peer in range(peers):
        part = peer // (peers * share // row_count)
        rows = small_ref.at[part * share : (part + 1) * share]
        copies.append(pltpu.make_async_copy(rows, out_hbm.at[peer], sems.at[4 + parts + peer]))
    for copy in copies:
        copy.start()
    slab = spread(slab_ref, 0, slab_count, rows_of((slab_count, LANES)))
    for a in range(row_count):
        left_ref[a * slab_count : (a + 1) * slab_count, :] = slab ^ virt_ref[va * row_count + a]
    for copy in copies:
        copy.wait()
    bring.wait()


def squeeze_amp_kernel(pair_ref, left_ref, amp_ref, out_ref):
    width = amp_ref.shape[1]
    left = left_ref[...]
    step = GROUP * LANES
    squeeze = squeezer(step)
    for part in range(width // step):
        kept = []
        for block in range(GROUP):
            at = part * GROUP + block
            held = amp_ref[:, at * LANES : (at + 1) * LANES].astype(F32)
            kept.append(jnp.where(left == pair_ref[at : at + 1, :], held, 0.0).astype(BF16))
        small = jnp.dot(jnp.concatenate(kept, 1), squeeze, preferred_element_type=F32)
        out_ref[:, part * LANES : (part + 1) * LANES] = small.astype(BF16)


def sort_keys(labels):
    at = lanes(labels.shape)
    return (at // RUN) * (RUN * GROUP) + labels * RUN + at % RUN


def column_tags(va, virt_ref, slab_ref, occ_ref, a_count):
    slab_count = slab_ref.shape[0]
    at = lanes((1, a_count * slab_count))
    first = spread(virt_ref, va * a_count, a_count, at // slab_count)
    return first ^ spread(slab_ref, 0, slab_count, at % slab_count) ^ occ_ref[0]


def plan_kernel(
    a_count, va_axes, vb_axes, virt_ref, occ_ref, slab_ref, labels_ref,
    move_ref, tag_ref, columns_ref, place_ref, label_ref, most_ref,
):
    share = lax.axis_index("xl")
    va, vb = first_of(va_axes), first_of(vb_axes)
    across = va_axes[1][1] * va_axes[2][1]
    partner = va + (1 - 2 * share) * across
    for side, at in enumerate((va, partner)):
        tags = column_tags(at, virt_ref, slab_ref, occ_ref, a_count)
        columns_ref[8 * side : 8 * side + 8, :] = jnp.broadcast_to(tags, (8, tags.shape[1]))
    labels = labels_ref[...]
    run = lanes(labels.shape) // RUN
    most = jnp.int32(0)
    for label in range(GROUP):
        for side in range(LANES // RUN):
            hits = jnp.where((labels == label) & (run == side), 1.0, 0.0)
            most = jnp.maximum(most, jnp.max(jnp.sum(hits, axis=1, keepdims=True)).astype(I32))
    most_ref[0] = most

    count = labels.shape[0] // 2
    mine = jnp.where(share == 0, labels[:count], labels[count:])
    mine = jnp.concatenate([mine, mine], 0)
    keys_across, labels_across = sort_keys(mine).astype(F32), mine.astype(F32)
    keys_down = jnp.transpose(keys_across)
    square = (LANES, LANES)
    for r in range(count):
        before = jnp.where(keys_down[:, r : r + 1] < keys_across[r : r + 1, :], 1.0, 0.0)
        place = jnp.sum(before, axis=0, keepdims=True)
        moved = jnp.where(rows_of(square).astype(F32) == place, 1.0, 0.0)
        move_ref[r] = moved.astype(BF16)
        tag_ref[r * LANES : (r + 1) * LANES, :] = jnp.broadcast_to(
            jnp.sum(moved * labels_across[r : r + 1, :], axis=1, keepdims=True), square
        ).astype(I32)

    per = LANES // RUN
    for part in range(2):
        row = labels_ref[pl.ds(part * count + vb // per, 1), :]
        held = lanes(row.shape) // RUN == vb % per
        key = jnp.where(held, row * RUN + lanes(row.shape) % RUN, RUN * GROUP).astype(F32)
        on_own = rows_of((RUN, LANES)) == jnp.where(held, lanes(row.shape) % RUN, -1)
        key_down = jnp.sum(jnp.where(on_own, key, 0.0), axis=1, keepdims=True)
        label_down = jnp.sum(jnp.where(on_own, row.astype(F32), 0.0), axis=1, keepdims=True)
        place = jnp.sum(jnp.where(key < key_down, 1.0, 0.0), axis=1, keepdims=True)
        place_ref[part * RUN : (part + 1) * RUN, :] = jnp.broadcast_to(place, (RUN, LANES)).astype(I32)
        label_ref[part * RUN : (part + 1) * RUN, :] = jnp.broadcast_to(label_down, (RUN, label_ref.shape[1])).astype(I32)


def folded(part, span):
    count = part.shape[0]
    if span > count:
        return jnp.concatenate([part, jnp.zeros((span - count, part.shape[1]), F32)], 0)
    slots = span - 1
    row = rows_of((span, part.shape[1]))
    total = jnp.where(row < slots, part[:span], 0.0)
    for low in range(slots, count, slots):
        moved = pltpu.roll(part, count - low, 0)[:span]
        total = total + jnp.where(row < min(slots, count - low), moved, 0.0)
    return total


def multiply_kernel(span, move_ref, tag_ref, columns_ref, rows_ref, amp_ref, partner_ref, out_ref, sorted_ref):
    cores, windows = rows_ref.shape[:2]
    per = LANES // RUN
    halves = amp_ref.shape[0] // LANES
    share = lax.axis_index("xl")
    for r in range(windows // per):
        block = jnp.concatenate([x for w in range(r * per, (r + 1) * per) for x in [rows_ref[core, w] for core in range(cores)]], 0)
        sorted_ref[r * LANES : (r + 1) * LANES, :] = jnp.dot(
            move_ref[r], block, preferred_element_type=F32
        ).astype(BF16)
    for side, columns_of in enumerate((amp_ref, partner_ref)):
        first = (share if side == 0 else 1 - share) * windows
        for r in range(windows // per):
            at = slice(r * LANES, (r + 1) * LANES)
            sums = lax.dot_general(
                sorted_ref[at, :], columns_of[...], (((1,), (1,)), ((), ())), preferred_element_type=F32
            )
            tags = jnp.concatenate([tag_ref[at, :]] * halves, 1)
            sums = jnp.where(tags == columns_ref[8 * side : 8 * side + 1, :], sums, 0.0)
            for w in range(per):
                total = folded(sums[w * RUN : (w + 1) * RUN], span)
                largest = jnp.max(jnp.max(jnp.abs(total), axis=0, keepdims=True), axis=1, keepdims=True)
                power = jnp.ceil(jnp.log2(jnp.maximum(largest, SMALLEST)))
                total = total * jnp.exp2(TOP - power)
                code = total * jnp.abs(total)
                square = total * total
                for _ in range(ROOTS - 1):
                    code, square = code * square, square * square
                code = jnp.where(rows_of(code.shape) == span - 1, power, code).astype(BF16)
                for half in range(halves):
                    out_ref[first + r * per + w, half * span : (half + 1) * span, :] = code[:, half * LANES : (half + 1) * LANES]


def finish_kernel(span, columns_ref, place_ref, label_ref, parts_ref, out_ref):
    halves = out_ref.shape[1] // LANES
    sources = parts_ref.shape[0] // 2
    slots = span - 1
    for part in range(2):
        totals = []
        for half in range(halves):
            total = jnp.zeros((span, LANES), F32)
            for source in range(sources):
                code = parts_ref[part * sources + source, half * span : (half + 1) * span, :].astype(F32)
                root = jnp.exp2(jnp.log2(jnp.abs(code)) * 0.5**ROOTS)
                total = total + jnp.where(code < 0.0, -root, root) * jnp.exp2(code[span - 1 :, :] - TOP)
            totals.append(total)
        at = slice(part * RUN, (part + 1) * RUN)
        place = place_ref[at, 0:1]
        slot = jnp.where(place >= 2 * slots, place - 2 * slots, jnp.where(place >= slots, place - slots, place))
        chosen = jnp.where(lanes((RUN, span)) == slot, 1.0, 0.0).astype(BF16)
        full = jnp.dot(chosen, jnp.concatenate(totals, 1).astype(BF16), preferred_element_type=F32)
        full = jnp.where(label_ref[at, :] == columns_ref[0:1, :], full, 0.0).astype(BF16)
        half_run = RUN // 2
        for core in range(2):
            low = core * RUN + part * half_run
            out_ref[low : low + half_run, :] = full[core * half_run : (core + 1) * half_run]


def per_device(sizes, amplitudes, integrals, irrep_virt, irrep_occ, irrep_slab):
    va_axes = [(name, sizes[name]) for name in ("xl", "y", "c")]
    vb_axes = [(name, sizes[name]) for name in ("xh", "z")]
    a_rows, slab_count, width = amplitudes.shape
    b_rows = integrals.shape[0]
    depth = width // GROUP
    chips = sizes["xl"] * sizes["y"]
    columns = a_rows * slab_count
    shaped = jax.ShapeDtypeStruct
    share = b_rows // sizes["xl"]

    arrays = (irrep_virt, irrep_occ, irrep_slab, integrals, amplitudes.reshape(columns, width))
    small, amp_near, pair_tag, left_tag = pl.pallas_call(
        functools.partial(squeeze_int_kernel, va_axes, vb_axes),
        out_shape=(
            shaped((chips, share, depth), BF16),
            shaped((columns, width), BF16),
            shaped((width // LANES, LANES), I32),
            shaped((columns, LANES), I32),
        ),
        in_specs=[HBM] * 5,
        out_specs=(ANY, VMEM, VMEM, VMEM),
        scratch_shapes=[
            pltpu.SMEM(irrep_virt.shape, I32),
            pltpu.SMEM(irrep_occ.shape, I32),
            pltpu.SMEM(irrep_slab.shape, I32),
            pltpu.VMEM((b_rows, width), BF16),
            pltpu.VMEM((b_rows, depth), BF16),
            pltpu.SemaphoreType.DMA((4 + width // (GROUP * LANES) + chips,)),
        ],
        compiler_params=params(),
        name="squeeze_int",
    )(*(pltpu.with_memory_space_constraint(x, pltpu.HBM) for x in arrays))
    own = lax.all_to_all(small, ("xl", "y"), 0, 0, tiled=False)

    amp_small = pl.pallas_call(
        squeeze_amp_kernel,
        out_shape=shaped((columns, depth), BF16),
        in_specs=[VMEM] * 3,
        out_specs=VMEM,
        compiler_params=params(),
        cost_estimate=pl.CostEstimate(flops=4 << 30, transcendentals=0, bytes_accessed=8 << 20),
        name="squeeze_amp",
    )(pair_tag, left_tag, amp_near)
    amp_partner = lax.ppermute(amp_small, "xl", [(0, 1), (1, 0)])

    labels = irrep_virt.reshape(chips, sizes["c"], sizes["xl"], share).transpose(2, 0, 1, 3).reshape(-1, LANES)
    *plan, most = pl.pallas_call(
        functools.partial(plan_kernel, a_rows, va_axes, vb_axes),
        out_shape=(
            shaped((labels.shape[0] // 2, LANES, LANES), BF16),
            shaped((labels.size // 2, LANES), I32),
            shaped((16, columns), I32),
            shaped((WINDOW, LANES), I32),
            shaped((WINDOW, columns), I32),
            shaped((1,), I32),
        ),
        in_specs=[SMEM, SMEM, SMEM, VMEM],
        out_specs=(VMEM,) * 5 + (SMEM,),
        compiler_params=params(),
        cost_estimate=pl.CostEstimate(flops=2 << 30, transcendentals=0, bytes_accessed=4 << 20),
        name="plan",
    )(irrep_virt, irrep_occ, irrep_slab, labels)

    def rest(span, move, tags, column_labels, place, row_labels, both, amp_small, amp_partner):
        parts = pl.pallas_call(
            functools.partial(multiply_kernel, span),
            out_shape=shaped((2 * chips, columns // LANES * span, LANES), BF16),
            in_specs=[VMEM] * 6,
            out_specs=VMEM,
            scratch_shapes=[pltpu.VMEM((chips * RUN, depth), BF16)],
            compiler_params=params(),
            name="multiply",
        )(move, tags, column_labels, both, amp_small, amp_partner)
        parts = lax.all_to_all(parts, ("xl", "xh", "z"), 0, 0, tiled=False)
        return pl.pallas_call(
            functools.partial(finish_kernel, span),
            out_shape=shaped((WINDOW, columns), BF16),
            in_specs=[VMEM] * 4,
            out_specs=VMEM,
            compiler_params=params(),
            name="finish",
        )(column_labels, place, row_labels, parts)

    tier = sum((most[0] >= span).astype(I32) for span in SPANS)
    own, amp_small, tier, *plan = lax.optimization_barrier((own, amp_small, tier, *plan))
    both = lax.all_gather(own, "c", axis=0, tiled=False)

    return lax.switch(
        tier,
        [functools.partial(rest, span) for span in (*SPANS, RUN + 8)],
        *plan, both, amp_small, amp_partner,
    )


def solution(mesh):
    names = ("xl", "y", "c", "xh", "z")
    shape = (2, mesh.shape["va"] // 4, 2, 2, mesh.shape["vb"] // 2)
    fine = Mesh(mesh.devices.reshape(shape), names)
    va, vb = names[:3], names[3:]
    return jax.shard_map(
        functools.partial(per_device, dict(zip(names, shape))),
        mesh=fine,
        in_specs=(P(va, None, vb), P(va, vb), P(), P(), P()),
        out_specs=P(vb, va),
        check_vma=False,
    )
```

```python
import functools

import jax
import jax.numpy as jnp
from jax import lax
from jax.experimental import pallas as pl
from jax.experimental.pallas import tpu as pltpu
from jax.sharding import Mesh, PartitionSpec as P

GROUP = 8
LANES = 128
ROOTS = 4
TOP = 7.0
SMALLEST = 2.0**-100
WINDOW = 64
RUN = 32
SPANS = (12, 16)

F32, BF16, I32 = jnp.float32, jnp.bfloat16, jnp.int32
SMEM = pl.BlockSpec(memory_space=pltpu.SMEM)
VMEM = pl.BlockSpec(memory_space=pltpu.VMEM)
HBM = pl.BlockSpec(memory_space=pltpu.HBM)
ANY = pl.BlockSpec(memory_space=pl.ANY)


def params(**more):
    return pltpu.CompilerParams(vmem_limit_bytes=48 << 20, **more)


def lanes(shape):
    return lax.broadcasted_iota(I32, shape, len(shape) - 1)


def rows_of(shape):
    return lax.broadcasted_iota(I32, shape, len(shape) - 2)


def spread(ref, start, count, position):
    out = jnp.zeros_like(position)
    for n in range(count):
        out = jnp.where(position == n, ref[start + n], out)
    return out


def occ_lanes(occ_ref):
    occ_count = occ_ref.shape[0]
    return spread(occ_ref, 0, occ_count, lanes((1, LANES)) % occ_count)


def pair_tags(occ, virt_ref, first_c, block, occ_count):
    per = LANES // occ_count
    c_of = lanes((1, LANES)) // occ_count
    return occ ^ spread(virt_ref, first_c + block * per, per, c_of)


def squeezer(width):
    shape = (width, width // GROUP)
    return jnp.where(rows_of(shape) // GROUP == lanes(shape), 1.0, 0.0).astype(BF16)


def first_of(axis_sizes):
    at = 0
    for name, size in axis_sizes:
        at = at * size + lax.axis_index(name)
    return at


def squeeze_int_kernel(
    va_axes, vb_axes, virt_hbm, occ_hbm, slab_hbm, int_hbm, amp_hbm, out_hbm, amp_ref, pair_ref, left_ref,
    virt_ref, occ_ref, slab_ref, int_ref, small_ref, sems,
):
    row_count, width = int_ref.shape
    occ_count, slab_count = occ_ref.shape[0], slab_ref.shape[0]
    c_count = width // occ_count
    step = GROUP * LANES
    parts = width // step
    fetch = [
        pltpu.make_async_copy(virt_hbm, virt_ref, sems.at[0]),
        pltpu.make_async_copy(occ_hbm, occ_ref, sems.at[1]),
        pltpu.make_async_copy(slab_hbm, slab_ref, sems.at[2]),
    ]
    for part in range(parts):
        span = pl.ds(part * step, step)
        fetch.append(pltpu.make_async_copy(int_hbm.at[:, span], int_ref.at[:, span], sems.at[4 + part]))
    bring = pltpu.make_async_copy(amp_hbm, amp_ref, sems.at[3])
    for copy in fetch:
        copy.start()
    bring.start()
    va, vb = first_of(va_axes), first_of(vb_axes)
    squeeze = squeezer(step)
    for copy in fetch[:3]:
        copy.wait()
    occ = occ_lanes(occ_ref)
    row_tag = spread(virt_ref, va * row_count, row_count, rows_of((row_count, LANES))) ^ occ_ref[0]
    stacked = []
    for part in range(parts):
        fetch[3 + part].wait()
        kept = []
        for block in range(GROUP):
            at = part * GROUP + block
            tag = pair_tags(occ, virt_ref, vb * c_count, at, occ_count)
            pair_ref[at : at + 1, :] = tag
            held = int_ref[:, at * LANES : (at + 1) * LANES].astype(F32)
            kept.append(jnp.where(row_tag == tag, held, 0.0).astype(BF16))
        stacked.append(jnp.concatenate(kept, 1))
    small = jnp.dot(jnp.concatenate(stacked, 0), squeeze, preferred_element_type=F32).astype(BF16)
    for part in range(parts):
        small_ref[:, part * LANES : (part + 1) * LANES] = small[part * row_count : (part + 1) * row_count]
    peers, share = out_hbm.shape[0], out_hbm.shape[1]
    copies = []
    for peer in range(peers):
        part = peer // (peers * share // row_count)
        rows = small_ref.at[part * share : (part + 1) * share]
        copies.append(pltpu.make_async_copy(rows, out_hbm.at[peer], sems.at[4 + parts + peer]))
    for copy in copies:
        copy.start()
    slab = spread(slab_ref, 0, slab_count, rows_of((slab_count, LANES)))
    for a in range(row_count):
        left_ref[a * slab_count : (a + 1) * slab_count, :] = slab ^ virt_ref[va * row_count + a]
    for copy in copies:
        copy.wait()
    bring.wait()


def squeeze_amp_kernel(pair_ref, left_ref, amp_ref, out_ref):
    width = amp_ref.shape[1]
    left = left_ref[...]
    step = GROUP * LANES
    squeeze = squeezer(step)
    for part in range(width // step):
        kept = []
        for block in range(GROUP):
            at = part * GROUP + block
            held = amp_ref[:, at * LANES : (at + 1) * LANES].astype(F32)
            kept.append(jnp.where(left == pair_ref[at : at + 1, :], held, 0.0).astype(BF16))
        small = jnp.dot(jnp.concatenate(kept, 1), squeeze, preferred_element_type=F32)
        out_ref[:, part * LANES : (part + 1) * LANES] = small.astype(BF16)


def sort_keys(labels):
    at = lanes(labels.shape)
    return (at // RUN) * (RUN * GROUP) + labels * RUN + at % RUN


def column_tags(va, virt_ref, slab_ref, occ_ref, a_count):
    slab_count = slab_ref.shape[0]
    at = lanes((1, a_count * slab_count))
    first = spread(virt_ref, va * a_count, a_count, at // slab_count)
    return first ^ spread(slab_ref, 0, slab_count, at % slab_count) ^ occ_ref[0]


def plan_kernel(
    a_count, va_axes, vb_axes, virt_ref, occ_ref, slab_ref, labels_ref,
    move_ref, tag_ref, columns_ref, place_ref, label_ref, most_ref,
):
    share = lax.axis_index("xl")
    va, vb = first_of(va_axes), first_of(vb_axes)
    across = va_axes[1][1] * va_axes[2][1]
    partner = va + (1 - 2 * share) * across
    for side, at in enumerate((va, partner)):
        tags = column_tags(at, virt_ref, slab_ref, occ_ref, a_count)
        columns_ref[8 * side : 8 * side + 8, :] = jnp.broadcast_to(tags, (8, tags.shape[1]))
    labels = labels_ref[...]
    run = lanes(labels.shape) // RUN
    most = jnp.int32(0)
    for label in range(GROUP):
        for side in range(LANES // RUN):
            hits = jnp.where((labels == label) & (run == side), 1.0, 0.0)
            most = jnp.maximum(most, jnp.max(jnp.sum(hits, axis=1, keepdims=True)).astype(I32))
    most_ref[0] = most

    count = labels.shape[0] // 2
    mine = jnp.where(share == 0, labels[:count], labels[count:])
    mine = jnp.concatenate([mine, mine], 0)
    keys_across, labels_across = sort_keys(mine).astype(F32), mine.astype(F32)
    keys_down = jnp.transpose(keys_across)
    square = (LANES, LANES)
    for r in range(count):
        before = jnp.where(keys_down[:, r : r + 1] < keys_across[r : r + 1, :], 1.0, 0.0)
        place = jnp.sum(before, axis=0, keepdims=True)
        moved = jnp.where(rows_of(square).astype(F32) == place, 1.0, 0.0)
        move_ref[r] = moved.astype(BF16)
        tag_ref[r * LANES : (r + 1) * LANES, :] = jnp.broadcast_to(
            jnp.sum(moved * labels_across[r : r + 1, :], axis=1, keepdims=True), square
        ).astype(I32)

    per = LANES // RUN
    for part in range(2):
        row = labels_ref[pl.ds(part * count + vb // per, 1), :]
        held = lanes(row.shape) // RUN == vb % per
        key = jnp.where(held, row * RUN + lanes(row.shape) % RUN, RUN * GROUP).astype(F32)
        on_own = rows_of((RUN, LANES)) == jnp.where(held, lanes(row.shape) % RUN, -1)
        key_down = jnp.sum(jnp.where(on_own, key, 0.0), axis=1, keepdims=True)
        label_down = jnp.sum(jnp.where(on_own, row.astype(F32), 0.0), axis=1, keepdims=True)
        place = jnp.sum(jnp.where(key < key_down, 1.0, 0.0), axis=1, keepdims=True)
        place_ref[part * RUN : (part + 1) * RUN, :] = jnp.broadcast_to(place, (RUN, LANES)).astype(I32)
        label_ref[part * RUN : (part + 1) * RUN, :] = jnp.broadcast_to(label_down, (RUN, label_ref.shape[1])).astype(I32)


def folded(part, span):
    count = part.shape[0]
    if span > count:
        return jnp.concatenate([part, jnp.zeros((span - count, part.shape[1]), F32)], 0)
    slots = span - 1
    row = rows_of((span, part.shape[1]))
    total = jnp.where(row < slots, part[:span], 0.0)
    for low in range(slots, count, slots):
        moved = pltpu.roll(part, count - low, 0)[:span]
        total = total + jnp.where(row < min(slots, count - low), moved, 0.0)
    return total


def masked_sums(rows, columns_of, tags, columns):
    sums = lax.dot_general(rows, columns_of, (((1,), (1,)), ((), ())), preferred_element_type=F32)
    return jnp.where(jnp.concatenate([tags] * (sums.shape[1] // LANES), 1) == columns, sums, 0.0)


def multiply_own_kernel(move_ref, tag_ref, columns_ref, rows_ref, amp_ref, sorted_ref, sums_ref):
    cores, windows = rows_ref.shape[:2]
    per = LANES // RUN
    for r in range(windows // per):
        block = jnp.concatenate([rows_ref[core, w] for w in range(r * per, (r + 1) * per) for core in range(cores)], 0)
        sorted_ref[r * LANES : (r + 1) * LANES, :] = jnp.dot(
            move_ref[r], block, preferred_element_type=F32
        ).astype(BF16)
    for r in range(windows // per):
        at = slice(r * LANES, (r + 1) * LANES)
        sums_ref[at, :] = masked_sums(sorted_ref[at, :], amp_ref[...], tag_ref[at, :], columns_ref[0:1, :])


def multiply_kernel(span, tag_ref, columns_ref, sorted_ref, own_ref, partner_ref, out_ref):
    windows = sorted_ref.shape[0] // RUN
    per = LANES // RUN
    halves = partner_ref.shape[0] // LANES
    share = lax.axis_index("xl")
    for side in range(2):
        first = (share if side == 0 else 1 - share) * windows
        for r in range(windows // per):
            at = slice(r * LANES, (r + 1) * LANES)
            if side == 0:
                sums = own_ref[at, :]
            else:
                sums = masked_sums(sorted_ref[at, :], partner_ref[...], tag_ref[at, :], columns_ref[8:9, :])
            for w in range(per):
                total = folded(sums[w * RUN : (w + 1) * RUN], span)
                largest = jnp.max(jnp.max(jnp.abs(total), axis=0, keepdims=True), axis=1, keepdims=True)
                power = jnp.ceil(jnp.log2(jnp.maximum(largest, SMALLEST)))
                total = total * jnp.exp2(TOP - power)
                code = total * jnp.abs(total)
                square = total * total
                for _ in range(ROOTS - 1):
                    code, square = code * square, square * square
                code = jnp.where(rows_of(code.shape) == span - 1, power, code).astype(BF16)
                for half in range(halves):
                    out_ref[first + r * per + w, half * span : (half + 1) * span, :] = code[:, half * LANES : (half + 1) * LANES]


def finish_kernel(span, columns_ref, place_ref, label_ref, parts_ref, out_ref):
    halves = out_ref.shape[1] // LANES
    sources = parts_ref.shape[0] // 2
    slots = span - 1
    for part in range(2):
        totals = []
        for half in range(halves):
            total = jnp.zeros((span, LANES), F32)
            for source in range(sources):
                code = parts_ref[part * sources + source, half * span : (half + 1) * span, :].astype(F32)
                root = jnp.exp2(jnp.log2(jnp.abs(code)) * 0.5**ROOTS)
                total = total + jnp.where(code < 0.0, -root, root) * jnp.exp2(code[span - 1 :, :] - TOP)
            totals.append(total)
        at = slice(part * RUN, (part + 1) * RUN)
        place = place_ref[at, 0:1]
        slot = jnp.where(place >= 2 * slots, place - 2 * slots, jnp.where(place >= slots, place - slots, place))
        chosen = jnp.where(lanes((RUN, span)) == slot, 1.0, 0.0).astype(BF16)
        full = jnp.dot(chosen, jnp.concatenate(totals, 1).astype(BF16), preferred_element_type=F32)
        full = jnp.where(label_ref[at, :] == columns_ref[0:1, :], full, 0.0).astype(BF16)
        half_run = RUN // 2
        for core in range(2):
            low = core * RUN + part * half_run
            out_ref[low : low + half_run, :] = full[core * half_run : (core + 1) * half_run]


def per_device(sizes, amplitudes, integrals, irrep_virt, irrep_occ, irrep_slab):
    va_axes = [(name, sizes[name]) for name in ("xl", "y", "c")]
    vb_axes = [(name, sizes[name]) for name in ("xh", "z")]
    a_rows, slab_count, width = amplitudes.shape
    b_rows = integrals.shape[0]
    depth = width // GROUP
    chips = sizes["xl"] * sizes["y"]
    columns = a_rows * slab_count
    shaped = jax.ShapeDtypeStruct
    share = b_rows // sizes["xl"]

    arrays = (irrep_virt, irrep_occ, irrep_slab, integrals, amplitudes.reshape(columns, width))
    small, amp_near, pair_tag, left_tag = pl.pallas_call(
        functools.partial(squeeze_int_kernel, va_axes, vb_axes),
        out_shape=(
            shaped((chips, share, depth), BF16),
            shaped((columns, width), BF16),
            shaped((width // LANES, LANES), I32),
            shaped((columns, LANES), I32),
        ),
        in_specs=[HBM] * 5,
        out_specs=(ANY, VMEM, VMEM, VMEM),
        scratch_shapes=[
            pltpu.SMEM(irrep_virt.shape, I32),
            pltpu.SMEM(irrep_occ.shape, I32),
            pltpu.SMEM(irrep_slab.shape, I32),
            pltpu.VMEM((b_rows, width), BF16),
            pltpu.VMEM((b_rows, depth), BF16),
            pltpu.SemaphoreType.DMA((4 + width // (GROUP * LANES) + chips,)),
        ],
        compiler_params=params(),
        name="squeeze_int",
    )(*(pltpu.with_memory_space_constraint(x, pltpu.HBM) for x in arrays))
    own = lax.all_to_all(small, ("xl", "y"), 0, 0, tiled=False)

    amp_small = pl.pallas_call(
        squeeze_amp_kernel,
        out_shape=shaped((columns, depth), BF16),
        in_specs=[VMEM] * 3,
        out_specs=VMEM,
        compiler_params=params(),
        cost_estimate=pl.CostEstimate(flops=4 << 30, transcendentals=0, bytes_accessed=8 << 20),
        name="squeeze_amp",
    )(pair_tag, left_tag, amp_near)
    amp_partner = lax.ppermute(amp_small, "xl", [(0, 1), (1, 0)])

    labels = irrep_virt.reshape(chips, sizes["c"], sizes["xl"], share).transpose(2, 0, 1, 3).reshape(-1, LANES)
    *plan, most = pl.pallas_call(
        functools.partial(plan_kernel, a_rows, va_axes, vb_axes),
        out_shape=(
            shaped((labels.shape[0] // 2, LANES, LANES), BF16),
            shaped((labels.size // 2, LANES), I32),
            shaped((16, columns), I32),
            shaped((WINDOW, LANES), I32),
            shaped((WINDOW, columns), I32),
            shaped((1,), I32),
        ),
        in_specs=[SMEM, SMEM, SMEM, VMEM],
        out_specs=(VMEM,) * 5 + (SMEM,),
        compiler_params=params(),
        cost_estimate=pl.CostEstimate(flops=2 << 30, transcendentals=0, bytes_accessed=4 << 20),
        name="plan",
    )(irrep_virt, irrep_occ, irrep_slab, labels)

    def rest(span, tags, column_labels, place, row_labels, rows, own_sums, amp_partner):
        parts = pl.pallas_call(
            functools.partial(multiply_kernel, span),
            out_shape=shaped((2 * chips, columns // LANES * span, LANES), BF16),
            in_specs=[VMEM] * 5,
            out_specs=VMEM,
            compiler_params=params(),
            name="multiply",
        )(tags, column_labels, rows, own_sums, amp_partner)
        parts = lax.all_to_all(parts, ("xl", "xh", "z"), 0, 0, tiled=False)
        return pl.pallas_call(
            functools.partial(finish_kernel, span),
            out_shape=shaped((WINDOW, columns), BF16),
            in_specs=[VMEM] * 4,
            out_specs=VMEM,
            compiler_params=params(),
            name="finish",
        )(column_labels, place, row_labels, parts)

    tier = sum((most[0] >= span).astype(I32) for span in SPANS)
    own, amp_small, tier, *plan = lax.optimization_barrier((own, amp_small, tier, *plan))
    both = lax.all_gather(own, "c", axis=0, tiled=False)
    move, tags, column_labels, place, row_labels = plan
    rows, own_sums = pl.pallas_call(
        multiply_own_kernel,
        out_shape=(shaped((chips * RUN, depth), BF16), shaped((chips * RUN, columns), F32)),
        in_specs=[VMEM] * 5,
        out_specs=(VMEM, VMEM),
        compiler_params=params(),
        cost_estimate=pl.CostEstimate(flops=2 << 30, transcendentals=0, bytes_accessed=4 << 20),
        name="multiply_own",
    )(move, tags, column_labels, both, amp_small)

    return lax.switch(
        tier,
        [functools.partial(rest, span) for span in (*SPANS, RUN + 8)],
        tags, column_labels, place, row_labels, rows, own_sums, amp_partner,
    )


def solution(mesh):
    names = ("xl", "y", "c", "xh", "z")
    shape = (2, mesh.shape["va"] // 4, 2, 2, mesh.shape["vb"] // 2)
    fine = Mesh(mesh.devices.reshape(shape), names)
    va, vb = names[:3], names[3:]
    return jax.shard_map(
        functools.partial(per_device, dict(zip(names, shape))),
        mesh=fine,
        in_specs=(P(va, None, vb), P(va, vb), P(), P(), P()),
        out_specs=P(vb, va),
        check_vma=False,
    )
```
